32 devices in a mesh: mod: 4 (over y, x), dp: 8 (over z, core).
Axes of the slice: x: 2, y: 2, z: 4, core: 2. Of those that a mesh axis runs over, the one named last changes fastest.
Arguments:
- tokens: bfloat16 [32768, 768], P(('mod', 'dp')), may hold values from -6 to 6
- token_order: int32 [32, 1024], P(('mod', 'dp')), may hold values from 0 to 1023, each once within a row
- item_ids: int32 [32, 1024], P(('mod', 'dp')), may hold values from 0 to 3, as said below
- step_blocks: int32 [32, 1024], P(('mod', 'dp')), may hold values from 0 to 1
- item_sets: int32 [32, 4], P(('mod', 'dp')), may hold values from 0 to 24
- action_mask: int32 [25, 4], replicated, may hold values 0 or 1
- cotangent: bfloat16 [32768, 768], P(('mod', 'dp')), may hold values from -6 to 6
- ln1_gain: bfloat16 [768], replicated, may hold values from 0.5 to 1.5
- ln1_bias: bfloat16 [768], replicated, may hold values from -2 to 2
- w_qkv: bfloat16 [768, 2304], replicated, may hold values from -0.21875 to 0.21875
- b_qv: bfloat16 [2, 768], replicated, may hold values from -2 to 2
- w_out: bfloat16 [768, 768], replicated, may hold values from -0.875 to 0.875
- b_out: bfloat16 [768], replicated, may hold values from -2 to 2
- ln2_gain: bfloat16 [768], replicated, may hold values from 0.5 to 1.5
- ln2_bias: bfloat16 [768], replicated, may hold values from -2 to 2
- w_up: bfloat16 [768, 3072], replicated, may hold values from -0.21875 to 0.21875
- b_up: bfloat16 [3072], replicated, may hold values from -2 to 2
- w_down: bfloat16 [3072, 768], replicated, may hold values from -0.109375 to 0.109375
- b_down: bfloat16 [768], replicated, may hold values from -2 to 2
Outputs:
- mixed_out: bfloat16 [32768, 768], P(('mod', 'dp'))
- token_grad: bfloat16 [32768, 768], P(('mod', 'dp'))
- grad_ln1_gain: float32 [768], replicated
- grad_ln1_bias: float32 [768], replicated
- grad_w_qkv: float32 [768, 2304], replicated
- grad_b_qv: float32 [2, 768], replicated
- grad_w_out: float32 [768, 768], replicated
- grad_b_out: float32 [768], replicated
- grad_ln2_gain: float32 [768], replicated
- grad_ln2_bias: float32 [768], replicated
- grad_w_up: float32 [768, 3072], replicated
- grad_b_up: float32 [3072], replicated
- grad_w_down: float32 [3072, 768], replicated
- grad_b_down: float32 [768], replicated
The draws below stay inside these ranges and needn't reach their ends.
Inputs may be any that keep to these rules, and one draw needn't show every extreme that they name: `item_ids`: item ids start at 0 and never fall along a shard's rows; a shard holds 2 to 4 items, each value on 256 to 600 neighbouring positions; some shard has an item of exactly 600 rows.
All inputs are finite; a program needn't handle non-finite values.
Results may differ from the reference program's by a relative error of at most 0.012.
Values may be sent and summed in bfloat16 or wider, within the bound.
No kernel may reach another device: no remote copies, remote signals or barrier semaphores. Data moves between devices by JAX's collectives and lax.ppermute only.
A program may use at most 256 MiB of HBM per device.

```python
import math
import jax
import jax.numpy as jnp
import numpy as np
from jax import lax

D = 768
HEADS = 12
HEAD_DIM = 64
FF = 3072
TOK_DEV = 1024
MODS = 4
SEG_UNIT = 256
ITEM_MOST = 600
DATASETS = 25
STEP_KINDS = 2
ITEMS = 4
SHARDS = 32
TOKENS = 32768
N_MOD = 4
N_DP = 8


def draw_item_ids(key, part):
    row_total = SHARDS
    slot_total = ITEMS
    count_key = jax.random.fold_in(key, 11)
    fill_key = jax.random.fold_in(key, 23)
    row_index = jnp.arange(row_total, dtype=jnp.int32)[:, None]
    fixed = row_index == 0
    candidate = jnp.arange(1, slot_total + 1, dtype=jnp.int32)[None, :]
    rest = TOK_DEV - jnp.where(fixed, ITEM_MOST, 0)
    others = candidate - jnp.where(fixed, 1, 0)
    feasible = (candidate >= 2) & (others * SEG_UNIT <= rest) & (rest <= others * ITEM_MOST)
    score = jax.random.randint(count_key, (row_total, slot_total), 0, 1 << 20)
    score = jnp.where(feasible, score, -1)
    score = jnp.where((row_index == row_total - 1) & feasible, candidate * (1 << 21), score)
    count = jnp.argmax(score, axis=1).astype(jnp.int32) + 1
    slot = jnp.arange(slot_total, dtype=jnp.int32)[None, :]
    active = slot < count[:, None]
    first_fixed = fixed & (slot == 0)
    lengths = jnp.where(active, jnp.where(first_fixed, ITEM_MOST, SEG_UNIT), 0).astype(jnp.int32)
    room = jnp.where(active & ~first_fixed, ITEM_MOST - SEG_UNIT, 0).astype(jnp.int32)
    remain = (TOK_DEV - jnp.sum(lengths, axis=1)).astype(jnp.int32)

    def add_one(step, state):
        lengths, room, remain = state
        pick = jax.random.randint(jax.random.fold_in(fill_key, step), (row_total, slot_total), 0, 1 << 20)
        pick = jnp.where(room > 0, pick, -1)
        chosen = jnp.argmax(pick, axis=1).astype(jnp.int32)
        added = ((slot == chosen[:, None]) & (remain > 0)[:, None] & (room > 0)).astype(jnp.int32)
        return (lengths + added, room - added, remain - jnp.sum(added, axis=1))
    lengths, room, remain = lax.fori_loop(0, TOK_DEV, add_one, (lengths, room, remain))
    ends = jnp.cumsum(lengths, axis=1)
    position = jnp.arange(TOK_DEV, dtype=jnp.int32)
    ids = jnp.sum((position[None, :, None] >= ends[:, None, :]).astype(jnp.int32), axis=2)
    return jnp.minimum(ids, count[:, None] - 1).astype(jnp.int32)


def plant(array, rng, low, top_value):
    longest = array.shape.index(max(array.shape))
    spots = []
    for shift in (0, 1):
        where = [jax.random.randint(jax.random.fold_in(rng, axis), (), 0, length) for axis, length in enumerate(array.shape)]
        where[longest] = (where[longest] + shift) % array.shape[longest]
        spots.append(tuple(where))
    return array.at[spots[0]].set(low).at[spots[1]].set(top_value)


def level_of(own_key, shape, cuts, low, largest):
    def one(dim, shards_of):
        heights = jax.random.uniform(jax.random.fold_in(jax.random.fold_in(own_key, 6), dim), (shards_of,), jnp.float32, low / len(cuts), largest / len(cuts))
        return jnp.repeat(jnp.exp(heights), shape[dim] // shards_of).reshape((-1,) + (1,) * (len(shape) - dim - 1))

    level = one(*cuts[0])
    for cut in cuts[1:]:
        level = level * one(*cut)
    return level


def rank_table(number_of, slope):
    portions = [(1 << 20) // math.isqrt(grade ** slope) + 1 for grade in range(1, number_of + 1)]
    scale = 1 + sum(portions) // (1 << 30)
    return np.cumsum(np.array([max(1, weight // scale) for weight in portions]))


def skewed_ids(own_key, dims, count, slope):
    table = rank_table(count, slope)
    ticket = jax.random.randint(jax.random.fold_in(own_key, 1), dims, 0, int(table[count - 1]))
    grade = jnp.searchsorted(jnp.asarray(table, jnp.int32), ticket, side="right")
    return jax.random.permutation(jax.random.fold_in(own_key, 2), count)[grade].astype(jnp.int32)


def scatter_about(rng, shape, scale, limit, cuts=(), kind=jnp.bfloat16):
    factor_of = level_of(rng, shape, cuts, -0.22, 0.18) if cuts else 1.0
    drawn = jax.random.normal(rng, shape, jnp.float32) * scale * factor_of
    return jnp.minimum(jnp.maximum(drawn, -limit), limit).astype(kind)


def setup_inputs(seed: int = 0) -> dict:
    seeds = jax.random.split(jax.random.key(seed), 20)
    tokens = scatter_about(seeds[0], (TOKENS, D), 1.0, 6.0, ((0, 32),))
    token_order = jax.vmap(lambda own: jax.random.permutation(own, TOK_DEV))(jax.random.split(seeds[1], SHARDS)).reshape((SHARDS, TOK_DEV)).astype(jnp.int32)
    item_ids = draw_item_ids(jax.random.fold_in(seeds[19], 71), 0)
    step_blocks = plant(jax.random.randint(seeds[3], (SHARDS, TOK_DEV), 0, STEP_KINDS), jax.random.fold_in(seeds[3], 1), 0, STEP_KINDS - 1).astype(jnp.int32)
    item_sets = plant(skewed_ids(seeds[4], (SHARDS, ITEMS), DATASETS, 2), jax.random.fold_in(seeds[4], 3), 0, DATASETS - 1).astype(jnp.int32)
    action_mask = plant((jax.random.randint(seeds[5], (DATASETS, MODS), 0, 3) < 2).astype(jnp.int32), jax.random.fold_in(seeds[5], 1), 0, 1)
    cotangent = scatter_about(seeds[6], (TOKENS, D), 1.0, 6.0, ((0, 32),))
    ln1_gain = jnp.clip(1.0 + 0.1 * jax.random.normal(seeds[7], (D,), jnp.float32), 0.5, 1.5).astype(jnp.bfloat16)
    ln1_bias = scatter_about(seeds[8], (D,), 0.3, 2.0)
    w_qkv = scatter_about(seeds[9], (D, 3 * D), D ** -0.5, 0.21875)
    b_qv = scatter_about(seeds[10], (2, D), 0.3, 2.0)
    w_out = scatter_about(seeds[11], (D, D), (D // 16) ** -0.5, 0.875)
    b_out = scatter_about(seeds[12], (D,), 0.3, 2.0)
    ln2_gain = jnp.clip(1.0 + 0.1 * jax.random.normal(seeds[13], (D,), jnp.float32), 0.5, 1.5).astype(jnp.bfloat16)
    ln2_bias = scatter_about(seeds[14], (D,), 0.3, 2.0)
    w_up = scatter_about(seeds[15], (D, FF), D ** -0.5, 0.21875)
    b_up = scatter_about(seeds[16], (FF,), 0.3, 2.0)
    w_down = scatter_about(seeds[17], (FF, D), FF ** -0.5, 0.109375)
    b_down = scatter_about(seeds[18], (D,), 0.3, 2.0)
    return dict(tokens=tokens, token_order=token_order, item_ids=item_ids, step_blocks=step_blocks, item_sets=item_sets, action_mask=action_mask, cotangent=cotangent, ln1_gain=ln1_gain, ln1_bias=ln1_bias, w_qkv=w_qkv, b_qv=b_qv, w_out=w_out, b_out=b_out, ln2_gain=ln2_gain, ln2_bias=ln2_bias, w_up=w_up, b_up=b_up, w_down=w_down, b_down=b_down)


LN_EPS = 1e-05
NEG_BIG = -1e+30

@jax.custom_vjp
def low(v):
    return lax.optimization_barrier(v.astype(jnp.bfloat16)).astype(jnp.float32)

@jax.custom_vjp
def low_back(v):
    return v

def low_keep(v):
    return (low(v), None)

def low_pass(kept, grad):
    return (grad,)

def back_keep(v):
    return (v, None)

def back_low(kept, grad):
    return (low(grad),)
low.defvjp(low_keep, low_pass)
low_back.defvjp(back_keep, back_low)

def layer_norm(values, gain, shift):
    center = values - lax.optimization_barrier(jnp.mean(values, axis=-1, keepdims=True))
    spread = lax.optimization_barrier(jnp.mean(center * center, axis=-1, keepdims=True))
    return center * lax.rsqrt(spread + LN_EPS) * gain + shift

def matmul(left, right):
    return jnp.dot(left, right, precision=lax.Precision.HIGHEST)

def shard_forward(params, parts):
    gain_one, shift_one, w_qkv, b_qv, w_out, b_out, gain_two, shift_two, w_up, b_up, w_down, b_down = params
    resid_in, segment, step_of = parts
    act_one = low(layer_norm(resid_in, gain_one, shift_one))
    qkv_all = matmul(act_one, w_qkv)
    query = low_back(low(qkv_all[:, :D] + b_qv[0]))
    keys_all = low_back(low(qkv_all[:, D:2 * D]))
    values_all = low_back(low(qkv_all[:, 2 * D:] + b_qv[1]))
    q_heads = query.reshape(TOK_DEV, HEADS, HEAD_DIM)
    k_heads = keys_all.reshape(TOK_DEV, HEADS, HEAD_DIM)
    v_heads = values_all.reshape(TOK_DEV, HEADS, HEAD_DIM)
    raw = low_back(HEAD_DIM ** (-0.5) * jnp.einsum('ihd,jhd->hij', q_heads, k_heads, precision=lax.Precision.HIGHEST))
    allowed = (segment[:, None] == segment[None, :]) & (step_of[None, :] <= step_of[:, None])
    prob = low(jax.nn.softmax(jnp.where(allowed[None], raw, NEG_BIG), axis=-1))
    attn_heads = jnp.einsum('hij,jhd->ihd', prob, v_heads, precision=lax.Precision.HIGHEST)
    attn_cat = low_back(low(attn_heads.reshape(TOK_DEV, D)))
    resid_mid = resid_in + low_back(matmul(attn_cat, w_out) + b_out)
    act_two = low(layer_norm(resid_mid, gain_two, shift_two))
    pre_hidden = low_back(matmul(act_two, w_up) + b_up)
    hidden = low(jax.nn.gelu(pre_hidden, approximate=True))
    return resid_mid + low_back(matmul(hidden, w_down) + b_down)

def reference(tokens, token_order, item_ids, step_blocks, item_sets, action_mask, cotangent, ln1_gain, ln1_bias, w_qkv, b_qv, w_out, b_out, ln2_gain, ln2_bias, w_up, b_up, w_down, b_down):
    shards = N_MOD * N_DP
    piece_rows = TOK_DEV // shards
    quarter_rows = TOK_DEV // N_MOD
    params = tuple((p.astype(jnp.float32) for p in (ln1_gain, ln1_bias, w_qkv, b_qv, w_out, b_out, ln2_gain, ln2_bias, w_up, b_up, w_down, b_down)))
    checked = jax.checkpoint(shard_forward)

    def forward(x_flat, weights):
        grid = x_flat.reshape(shards, shards, piece_rows, D).transpose(1, 0, 2, 3).reshape(shards, TOK_DEV, D)
        mixed = jax.vmap(lambda block, tok_order: jnp.take(block, tok_order, axis=0))(grid, token_order)
        return lax.map(lambda parts: checked(weights, parts), (mixed, item_ids, step_blocks))
    result, pull = jax.vjp(forward, tokens.astype(jnp.float32), params)
    set_row = jnp.take_along_axis(item_sets, item_ids, axis=1)
    modality = (token_order // quarter_rows).astype(jnp.int32)
    select = action_mask[set_row, modality].astype(jnp.float32)
    grad_y = cotangent.astype(jnp.float32).reshape(shards, TOK_DEV, D) * select[:, :, None]
    grad_x, grad_params = pull(grad_y)
    mixed_out = result.reshape(shards * TOK_DEV, D).astype(jnp.bfloat16)
    token_grad = grad_x.astype(jnp.bfloat16)
    g_one, s_one, g_qkv, g_bqv, g_out, g_bout, g_two, s_two, g_up, g_bup, g_down, g_bdown = grad_params
    return (mixed_out, token_grad, g_one, s_one, g_qkv, g_bqv, g_out, g_bout, g_two, s_two, g_up, g_bup, g_down, g_bdown)
```

```python
import functools

import jax
import jax.numpy as jnp
from jax import lax
from jax.experimental import pallas as pl
from jax.experimental.pallas import tpu as pltpu
from jax.sharding import PartitionSpec as P

HEAD_DIM = 64
LN_EPS = 1e-05
NEG_BIG = -1e30
F32 = jnp.float32
BF16 = jnp.bfloat16
AXES = ("mod", "dp")
WINDOWS = (512, 640, 768, 1024)
Q_ROWS = 256
ROW_BLOCK = 256
FF_BLOCK = 256
FF_PARTS = 2
HEAD_PARTS = 2
GELU_C = 0.7978845608028654
GELU_K = 0.044715


def dot_nn(left, right):
    return lax.dot_general(left, right, (((1,), (0,)), ((), ())), preferred_element_type=F32)


def dot_nt(left, right):
    return lax.dot_general(left, right, (((1,), (1,)), ((), ())), preferred_element_type=F32)


def cost(flops, moved, hard=0):
    return pl.CostEstimate(flops=flops, bytes_accessed=moved, transcendentals=hard)


def const_map(*_):
    return (0, 0)


def row_stats(values):
    mean = jnp.mean(values, axis=-1, keepdims=True)
    center = values - mean
    spread = jnp.mean(center * center, axis=-1, keepdims=True)
    return center, lax.rsqrt(spread + LN_EPS)


def norm_back(grad, hat, inv, gain):
    scaled = grad * gain
    return inv * (
        scaled
        - jnp.mean(scaled, axis=-1, keepdims=True)
        - hat * jnp.mean(scaled * hat, axis=-1, keepdims=True)
    )


def enter_kernel(order_ref, arr_ref, gain_ref, shift_ref, w_ref, bias_ref, x_ref, at_ref, qkv_ref):
    rows = arr_ref.shape[0]
    spots = lax.broadcasted_iota(jnp.int32, (order_ref.shape[0], rows), 1)
    hot = jnp.where(spots == order_ref[:, 0:1], 1.0, 0.0).astype(BF16)
    x = dot_nn(hot, arr_ref[...])
    x_ref[...] = x.astype(BF16)
    center, inv = row_stats(x)
    act = (center * inv * gain_ref[...] + shift_ref[...]).astype(BF16)
    at_ref[...] = act.T
    qkv_ref[...] = (dot_nn(act, w_ref[...]) + bias_ref[...]).astype(BF16)


def enter(order_col, arrived, gain, shift, w_qkv, bias):
    rows, width = arrived.shape
    triple = w_qkv.shape[1]
    blk = lambda i: (i, 0)
    return pl.pallas_call(
        enter_kernel,
        grid=(rows // ROW_BLOCK,),
        in_specs=[
            pl.BlockSpec((ROW_BLOCK, 128), blk),
            pl.BlockSpec((rows, width), const_map),
            pl.BlockSpec((1, width), const_map),
            pl.BlockSpec((1, width), const_map),
            pl.BlockSpec((width, triple), const_map),
            pl.BlockSpec((1, triple), const_map),
        ],
        out_specs=[
            pl.BlockSpec((ROW_BLOCK, width), blk),
            pl.BlockSpec((width, ROW_BLOCK), lambda i: (0, i)),
            pl.BlockSpec((ROW_BLOCK, triple), blk),
        ],
        out_shape=[
            jax.ShapeDtypeStruct((rows, width), BF16),
            jax.ShapeDtypeStruct((width, rows), BF16),
            jax.ShapeDtypeStruct((rows, triple), BF16),
        ],
        cost_estimate=cost(2 * rows * width * (triple + rows), 14 * rows * width),
        name="enter",
    )(order_col, arrived, gain, shift, w_qkv, bias)


def window_table(segment, rows):
    slots = jnp.arange(4, dtype=jnp.int32)
    starts = jnp.sum((segment[None, :] < slots[:, None]).astype(jnp.int32), axis=1)
    ends = jnp.sum((segment[None, :] <= slots[:, None]).astype(jnp.int32), axis=1)
    blocks = segment.reshape(rows // Q_ROWS, Q_ROWS)
    low = jnp.sum(jnp.where(blocks[:, :1] == slots[None, :], starts[None, :], 0), axis=1)
    high = jnp.sum(jnp.where(blocks[:, -1:] == slots[None, :], ends[None, :], 0), axis=1)
    start = (low // 128) * 128
    need = high - start
    wide = jnp.full_like(need, rows)
    for size in reversed(WINDOWS):
        wide = jnp.where(need <= size, size, wide)
    return jnp.stack([jnp.minimum(start, rows - wide), wide], axis=1).reshape(-1)


def lane_halves(block, scale=None):
    lane = lax.broadcasted_iota(jnp.int32, block.shape, 1)
    if scale is not None:
        block = block * jnp.asarray(scale, block.dtype)
    zero = jnp.zeros_like(block)
    return jnp.where(lane < HEAD_DIM, block, zero), jnp.where(lane < HEAD_DIM, zero, block)


def each_block(tab, rows, body):
    def block(b, carry):
        start, wide = tab[2 * b], tab[2 * b + 1]
        q_at = pl.multiple_of(b * Q_ROWS, Q_ROWS)
        k_at = pl.multiple_of(start, 128)
        for size in WINDOWS:
            pl.when(wide == size)(functools.partial(body, q_at, k_at, size))
        return carry

    lax.fori_loop(0, rows // Q_ROWS, block, 0)


def attend_kernel(tab, row_ref, col_ref, q_ref, k_ref, v_ref, o_ref, lse_ref, mask_ref):
    rows = q_ref.shape[0]

    @pl.when(pl.program_id(0) == 0)
    def _():
        key = row_ref[...]
        for r in range(0, rows, Q_ROWS):
            query = col_ref[r : r + Q_ROWS, 0:1]
            seen = (key <= query) & (key >= (query >> 1) * 2)
            mask_ref[r : r + Q_ROWS, :] = jnp.where(seen, 0.0, NEG_BIG)

    def one(q_at, k_at, size):
        halves = lane_halves(q_ref[pl.ds(q_at, Q_ROWS), :], HEAD_DIM**-0.5)
        keys = k_ref[pl.ds(k_at, size), :]
        vals = v_ref[pl.ds(k_at, size), :]
        outs, logs = [], []
        for half in halves:
            s = dot_nt(half, keys) + mask_ref[pl.ds(q_at, Q_ROWS), pl.ds(k_at, size)]
            top = jnp.max(s, axis=1, keepdims=True)
            e = jnp.exp(s - top)
            total = jnp.sum(e, axis=1, keepdims=True)
            outs.append(dot_nn(e.astype(BF16), vals) * (1.0 / total))
            logs.append(top + jnp.log(total))
        lane = lax.broadcasted_iota(jnp.int32, outs[0].shape, 1)
        o_ref[pl.ds(q_at, Q_ROWS), :] = jnp.where(lane < HEAD_DIM, outs[0], outs[1]).astype(BF16)
        stat = jnp.where(lane == 0, logs[0], logs[1])
        lse_ref[0, :, pl.ds(q_at, Q_ROWS)] = stat.T[0:2, :]

    each_block(tab, rows, one)


def attend(qkv, tab, code_row, code_col):
    rows = qkv.shape[0]
    width = qkv.shape[1] // 3
    pairs = width // 128
    return pl.pallas_call(
        attend_kernel,
        grid_spec=pltpu.PrefetchScalarGridSpec(
            num_scalar_prefetch=1,
            grid=(pairs,),
            in_specs=[
                pl.BlockSpec(code_row.shape, const_map),
                pl.BlockSpec(code_col.shape, const_map),
                pl.BlockSpec((rows, 128), lambda h, t: (0, h)),
                pl.BlockSpec((rows, 128), lambda h, t: (0, pairs + h)),
                pl.BlockSpec((rows, 128), lambda h, t: (0, 2 * pairs + h)),
            ],
            out_specs=[
                pl.BlockSpec((rows, 128), lambda h, t: (0, h)),
                pl.BlockSpec((1, 2, rows), lambda h, t: (h, 0, 0)),
            ],
            scratch_shapes=[pltpu.VMEM((rows, rows), F32)],
        ),
        out_shape=[
            jax.ShapeDtypeStruct((rows, width), BF16),
            jax.ShapeDtypeStruct((pairs, 2, rows), F32),
        ],
        cost_estimate=cost(16 * rows * rows * width, 8 * rows * width, 12 * rows * rows),
        name="attend",
    )(tab, code_row, code_col, qkv, qkv, qkv)


def attend_back_kernel(
    tab, row_ref, col_ref, q_ref, k_ref, v_ref, go_ref, lse_ref, g_ref, sum_ref, mask_ref, kt_ref, dk_ref, dv_ref
):
    rows = q_ref.shape[0]

    @pl.when(pl.program_id(0) == 0)
    def _():
        query = row_ref[...]
        low = (query >> 1) * 2
        for r in range(0, rows, Q_ROWS):
            key = col_ref[r : r + Q_ROWS, 0:1]
            seen = (key <= query) & (key >= low)
            mask_ref[r : r + Q_ROWS, :] = jnp.where(seen, 0.0, NEG_BIG)

    kt_ref[...] = k_ref[...].T
    dk_ref[...] = jnp.zeros_like(dk_ref)
    dv_ref[...] = jnp.zeros_like(dv_ref)

    def one(q_at, k_at, size):
        qs = pl.ds(q_at, Q_ROWS)
        ks = pl.ds(k_at, size)
        halves = lane_halves(q_ref[qs, :], HEAD_DIM**-0.5)
        grads = lane_halves(go_ref[qs, :])
        keys = k_ref[ks, :]
        vals = v_ref[ks, :]
        outs = []
        for h in range(2):
            s = dot_nt(keys, halves[h]) + mask_ref[ks, qs]
            p = jnp.exp(s - lse_ref[0, h : h + 1, qs])
            dp = dot_nt(vals, grads[h])
            delta = jnp.sum(p * dp, axis=0, keepdims=True)
            ds = (p * (dp - delta)).astype(BF16)
            dv_ref[ks, :] += dot_nn(p.astype(BF16), grads[h])
            dk_ref[ks, :] += dot_nn(ds, halves[h])
            outs.append(dot_nn(kt_ref[h * HEAD_DIM : (h + 1) * HEAD_DIM, ks], ds))
        dq = jnp.concatenate(outs, axis=0).T * HEAD_DIM**-0.5
        g_ref[0, qs, :] = dq.astype(BF16)

    each_block(tab, rows, one)
    g_ref[1] = dk_ref[...].astype(BF16)
    g_ref[2] = dv_ref[...].astype(BF16)
    sum_ref[0:1, :] = jnp.sum(g_ref[0].astype(F32), axis=0, keepdims=True)
    sum_ref[1:2, :] = jnp.sum(g_ref[2].astype(F32), axis=0, keepdims=True)


def attend_back(part, qkv, grad, lse, tab, code_row, code_col):
    rows = qkv.shape[0]
    width = qkv.shape[1] // 3
    pairs = width // 128
    count = pairs // HEAD_PARTS
    at = part * count
    share = count * 128
    return pl.pallas_call(
        attend_back_kernel,
        grid_spec=pltpu.PrefetchScalarGridSpec(
            num_scalar_prefetch=1,
            grid=(count,),
            in_specs=[
                pl.BlockSpec(code_row.shape, const_map),
                pl.BlockSpec(code_col.shape, const_map),
                pl.BlockSpec((rows, 128), lambda h, t: (0, at + h)),
                pl.BlockSpec((rows, 128), lambda h, t: (0, pairs + at + h)),
                pl.BlockSpec((rows, 128), lambda h, t: (0, 2 * pairs + at + h)),
                pl.BlockSpec((rows, 128), lambda h, t: (0, at + h)),
                pl.BlockSpec((1, 2, rows), lambda h, t: (at + h, 0, 0)),
            ],
            out_specs=[
                pl.BlockSpec((3, rows, 128), lambda h, t: (0, 0, h)),
                pl.BlockSpec((2, 128), lambda h, t: (0, h)),
            ],
            scratch_shapes=[
                pltpu.VMEM((rows, rows), F32),
                pltpu.VMEM((128, rows), BF16),
                pltpu.VMEM((rows, 128), F32),
                pltpu.VMEM((rows, 128), F32),
            ],
        ),
        out_shape=[
            jax.ShapeDtypeStruct((3, rows, share), BF16),
            jax.ShapeDtypeStruct((2, share), F32),
        ],
        cost_estimate=cost(40 * rows * rows * share, 14 * rows * share, 12 * rows * rows),
        name="attend_back",
    )(tab, code_row, code_col, qkv, qkv, qkv, grad, lse)


def middle_kernel(o_ref, x_ref, w_ref, b_ref, gain_ref, shift_ref, r_ref, at_ref):
    r = x_ref[...].astype(F32) + (dot_nn(o_ref[...], w_ref[...]) + b_ref[...])
    r_ref[...] = r
    center, inv = row_stats(r)
    at_ref[...] = (center * inv * gain_ref[...] + shift_ref[...]).astype(BF16).T


def middle(o, x, w_out, b_out, gain, shift):
    rows, width = x.shape
    blk = lambda i: (i, 0)
    vec = pl.BlockSpec((1, width), const_map)
    return pl.pallas_call(
        middle_kernel,
        grid=(rows // ROW_BLOCK,),
        in_specs=[
            pl.BlockSpec((ROW_BLOCK, width), blk),
            pl.BlockSpec((ROW_BLOCK, width), blk),
            pl.BlockSpec((width, width), const_map),
            vec,
            vec,
            vec,
        ],
        out_specs=[
            pl.BlockSpec((ROW_BLOCK, width), blk),
            pl.BlockSpec((width, ROW_BLOCK), lambda i: (0, i)),
        ],
        out_shape=[
            jax.ShapeDtypeStruct((rows, width), F32),
            jax.ShapeDtypeStruct((width, rows), BF16),
        ],
        cost_estimate=cost(2 * rows * width * width, 12 * rows * width),
        name="middle",
    )(o, x, w_out, b_out, gain, shift)


def branch_kernel(has_sum, at_ref, gd_ref, wut_ref, wd_ref, wu_ref, wdt_ref, bu_ref, *rest):
    if has_sum:
        y_in, g_in, y_ref, g_ref, gdown_ref, gup_ref, gb_ref = rest
    else:
        y_ref, g_ref, gdown_ref, gup_ref, gb_ref = rest

    @pl.when(pl.program_id(0) == 0)
    def _():
        if has_sum:
            y_ref[...] = y_in[...]
            g_ref[...] = g_in[...]
        else:
            y_ref[...] = jnp.zeros_like(y_ref)
            g_ref[...] = jnp.zeros_like(g_ref)

    act_t = at_ref[...]
    gd = gd_ref[...]
    u = dot_nn(wut_ref[...], act_t) + bu_ref[:, 0:1]
    square = u * u
    t = jnp.tanh(GELU_C * (u * (1.0 + GELU_K * square)))
    up = 0.5 * (1.0 + t)
    hidden = (u * up).astype(BF16)
    slope = up + (0.5 * GELU_C) * u * (1.0 - t * t) * (1.0 + (3.0 * GELU_K) * square)
    gu = (dot_nt(wd_ref[...], gd) * slope).astype(BF16)
    gdown_ref[...] = dot_nn(hidden, gd).astype(BF16)
    gup_ref[...] = dot_nt(act_t, gu).astype(BF16)
    y_ref[...] += dot_nn(wdt_ref[...], hidden)
    g_ref[...] += dot_nn(wu_ref[...], gu)
    gb_ref[...] = jnp.broadcast_to(jnp.sum(gu.astype(F32), axis=1, keepdims=True), gb_ref.shape)


def branch(part, act_t, gd, w_up_t, w_down, w_up, w_down_t, b_col, sums):
    width, rows = act_t.shape
    share = w_down.shape[0] // FF_PARTS
    steps = share // FF_BLOCK
    at = part * steps
    down = lambda c: (at + c, 0)
    across = lambda c: (0, at + c)
    whole = pl.BlockSpec((width, rows), const_map)
    return pl.pallas_call(
        functools.partial(branch_kernel, bool(sums)),
        grid=(steps,),
        in_specs=[
            whole,
            pl.BlockSpec((rows, width), const_map),
            pl.BlockSpec((FF_BLOCK, width), down),
            pl.BlockSpec((FF_BLOCK, width), down),
            pl.BlockSpec((width, FF_BLOCK), across),
            pl.BlockSpec((width, FF_BLOCK), across),
            pl.BlockSpec((FF_BLOCK, 128), down),
        ]
        + [whole] * len(sums),
        out_specs=[
            whole,
            whole,
            pl.BlockSpec((FF_BLOCK, width), lambda c: (c, 0)),
            pl.BlockSpec((width, FF_BLOCK), lambda c: (0, c)),
            pl.BlockSpec((FF_BLOCK, 128), lambda c: (c, 0)),
        ],
        out_shape=[
            jax.ShapeDtypeStruct((width, rows), F32),
            jax.ShapeDtypeStruct((width, rows), F32),
            jax.ShapeDtypeStruct((share, width), BF16),
            jax.ShapeDtypeStruct((width, share), BF16),
            jax.ShapeDtypeStruct((share, 128), F32),
        ],
        cost_estimate=cost(12 * rows * width * share, 20 * rows * width, rows * share),
        name="branch",
    )(act_t, gd, w_up_t, w_down, w_up, w_down_t, b_col, *sums)


def turn_kernel(yt_ref, gt_ref, r_ref, gd_ref, o_ref, w_ref, b_ref, gain_ref, mix_ref, gr_ref, go_ref, gw_ref, sum_ref, acc_ref):
    step = pl.program_id(0)

    @pl.when(step == 0)
    def _():
        acc_ref[...] = jnp.zeros_like(acc_ref)
        sum_ref[...] = jnp.zeros_like(sum_ref)

    r = r_ref[...]
    mix_ref[...] = (r + (yt_ref[...].T + b_ref[...])).astype(BF16)
    grad = gt_ref[...].T
    center, inv = row_stats(r)
    hat = center * inv
    gr = gd_ref[...].astype(F32) + norm_back(grad, hat, inv, gain_ref[...])
    gr_ref[...] = gr
    ga = gr.astype(BF16)
    go_ref[...] = dot_nt(ga, w_ref[...]).astype(BF16)
    acc_ref[...] += dot_nn(o_ref[...].T, ga)
    sum_ref[0:1, :] += jnp.sum(grad * hat, axis=0, keepdims=True)
    sum_ref[1:2, :] += jnp.sum(grad, axis=0, keepdims=True)
    sum_ref[2:3, :] += jnp.sum(ga.astype(F32), axis=0, keepdims=True)

    @pl.when(step == pl.num_programs(0) - 1)
    def _():
        gw_ref[...] = acc_ref[...].astype(BF16)


def turn(y_t, g_t, r, gd, o, w_out, b_down, gain):
    rows, width = r.shape
    blk = lambda i: (i, 0)
    across = lambda i: (0, i)
    row_spec = pl.BlockSpec((ROW_BLOCK, width), blk)
    vec = pl.BlockSpec((1, width), const_map)
    return pl.pallas_call(
        turn_kernel,
        grid=(rows // ROW_BLOCK,),
        in_specs=[
            pl.BlockSpec((width, ROW_BLOCK), across),
            pl.BlockSpec((width, ROW_BLOCK), across),
            row_spec,
            row_spec,
            row_spec,
            pl.BlockSpec((width, width), const_map),
            vec,
            vec,
        ],
        out_specs=[
            row_spec,
            row_spec,
            row_spec,
            pl.BlockSpec((width, width), const_map),
            pl.BlockSpec((8, width), const_map),
        ],
        out_shape=[
            jax.ShapeDtypeStruct((rows, width), BF16),
            jax.ShapeDtypeStruct((rows, width), F32),
            jax.ShapeDtypeStruct((rows, width), BF16),
            jax.ShapeDtypeStruct((width, width), BF16),
            jax.ShapeDtypeStruct((8, width), F32),
        ],
        scratch_shapes=[pltpu.VMEM((width, width), F32)],
        cost_estimate=cost(4 * rows * width * width, 24 * rows * width),
        name="turn",
    )(y_t, g_t, r, gd, o, w_out, b_down, gain)


def project_back_kernel(has_sum, at_ref, d_ref, w_ref, *rest):
    if has_sum:
        g_in, gw_ref, g_ref = rest
    else:
        gw_ref, g_ref = rest
    d = d_ref[0]
    gw_ref[0] = dot_nn(at_ref[...], d).astype(BF16)
    term = dot_nt(d, w_ref[...])

    @pl.when(pl.program_id(0) == 0)
    def _():
        if has_sum:
            g_ref[...] = g_in[...] + term
        else:
            g_ref[...] = term

    @pl.when(pl.program_id(0) > 0)
    def _():
        g_ref[...] += term


def project_back(part, act_t, d, w_qkv, sums):
    width, rows = act_t.shape
    share = d.shape[2]
    whole = pl.BlockSpec((rows, width), const_map)
    return pl.pallas_call(
        functools.partial(project_back_kernel, bool(sums)),
        grid=(3,),
        in_specs=[
            pl.BlockSpec((width, rows), const_map),
            pl.BlockSpec((1, rows, share), lambda i: (i, 0, 0)),
            pl.BlockSpec((width, share), lambda i: (0, HEAD_PARTS * i + part)),
        ]
        + [whole] * len(sums),
        out_specs=[pl.BlockSpec((1, width, share), lambda i: (i, 0, 0)), whole],
        out_shape=[
            jax.ShapeDtypeStruct((3, width, share), BF16),
            jax.ShapeDtypeStruct((rows, width), F32),
        ],
        cost_estimate=cost(12 * rows * width * share, 12 * rows * width),
        name="project_back",
    )(act_t, d, w_qkv, *sums)


def leave_kernel(order_ref, x_ref, g_ref, gr_ref, gain_ref, back_ref, sum_ref, gx_ref):
    step = pl.program_id(0)
    rows = back_ref.shape[0]

    @pl.when(step == 0)
    def _():
        sum_ref[...] = jnp.zeros_like(sum_ref)

    grad = g_ref[...]
    center, inv = row_stats(x_ref[...].astype(F32))
    hat = center * inv
    gx = gr_ref[...] + norm_back(grad, hat, inv, gain_ref[...])
    gx_ref[pl.ds(pl.multiple_of(step * ROW_BLOCK, ROW_BLOCK), ROW_BLOCK), :] = gx.astype(BF16)
    sum_ref[0:1, :] += jnp.sum(grad * hat, axis=0, keepdims=True)
    sum_ref[1:2, :] += jnp.sum(grad, axis=0, keepdims=True)

    @pl.when(step == pl.num_programs(0) - 1)
    def _():
        for r in range(0, rows, ROW_BLOCK):
            spots = lax.broadcasted_iota(jnp.int32, (ROW_BLOCK, rows), 0) + r
            hot = jnp.where(spots == order_ref[...], 1.0, 0.0).astype(BF16)
            back_ref[r : r + ROW_BLOCK, :] = dot_nn(hot, gx_ref[...]).astype(BF16)


def leave(order_row, x, grad, gr, gain):
    rows, width = x.shape
    row_spec = pl.BlockSpec((ROW_BLOCK, width), lambda i: (i, 0))
    return pl.pallas_call(
        leave_kernel,
        grid=(rows // ROW_BLOCK,),
        in_specs=[
            pl.BlockSpec((1, rows), const_map),
            row_spec,
            row_spec,
            row_spec,
            pl.BlockSpec((1, width), const_map),
        ],
        out_specs=[pl.BlockSpec((rows, width), const_map), pl.BlockSpec((8, width), const_map)],
        out_shape=[
            jax.ShapeDtypeStruct((rows, width), BF16),
            jax.ShapeDtypeStruct((8, width), F32),
        ],
        scratch_shapes=[pltpu.VMEM((rows, width), BF16)],
        cost_estimate=cost(2 * rows * rows * width, 12 * rows * width),
        name="leave",
    )(order_row, x, grad, gr, gain)


class Links:
    def __init__(self):
        inner = lax.axis_size("dp")
        self.total = lax.axis_size("mod") * inner
        self.me = lax.axis_index("mod") * inner + lax.axis_index("dp")
        low = range(1, inner.bit_length() - 1)
        high = range(inner.bit_length() - 1, self.total.bit_length() - 1)
        self.orders = ([0, *high, *low], [0, *reversed(high), *low])

    def swap(self, value, bit):
        pairs = [(i, i ^ (1 << bit)) for i in range(self.total)]
        return lax.ppermute(value, AXES, pairs)

    def side(self, bit):
        return (self.me >> bit) & 1

    def scatter_sum(self, value, axis, order):
        for bit in order:
            shape = value.shape
            cut = shape[:axis] + (2, shape[axis] // 2) + shape[axis + 1 :]
            halves = value.reshape(cut)
            mine = self.side(bit)
            send = lax.dynamic_index_in_dim(halves, 1 - mine, axis, keepdims=False).astype(BF16)
            keep = lax.dynamic_index_in_dim(halves, mine, axis, keepdims=False).astype(F32)
            value = keep + self.swap(send, bit).astype(F32)
        return value.astype(BF16)

    def gather(self, value, axis, order):
        for bit in reversed(order):
            other = self.swap(value, bit)
            shape = value.shape
            side = lax.broadcasted_iota(jnp.int32, shape[:axis] + (2,) + shape[axis:], axis)
            both = jnp.where(
                side == self.side(bit), jnp.expand_dims(value, axis), jnp.expand_dims(other, axis)
            )
            value = both.reshape(shape[:axis] + (2 * shape[axis],) + shape[axis + 1 :])
        return value

    def all_sum(self, value, axis, which):
        order = self.orders[which]
        return self.gather(self.scatter_sum(value, axis, order), axis, order)

    def small_sum(self, value):
        for bit in self.orders[0]:
            value = value + self.swap(value, bit)
        return value


def on_device(
    tokens,
    token_order,
    item_ids,
    step_blocks,
    item_sets,
    action_mask,
    cotangent,
    ln1_gain,
    ln1_bias,
    w_qkv,
    b_qv,
    w_out,
    b_out,
    ln2_gain,
    ln2_bias,
    w_up,
    b_up,
    w_down,
    b_down,
):
    rows, width = tokens.shape
    quarter_rows = rows // lax.axis_size("mod")
    links = Links()
    arrived = lax.all_to_all(tokens, AXES, split_axis=0, concat_axis=0, tiled=True)

    tok_order = token_order[0]
    segment = item_ids[0]
    code = segment * 2 + step_blocks[0]
    code_row = code[None, :]
    code_col = jnp.broadcast_to(code[:, None], (rows, 128))
    order_col = jnp.broadcast_to(tok_order[:, None], (rows, 128))
    tab = window_table(segment, rows)
    item_hot = segment[:, None] == jnp.arange(item_sets.shape[1], dtype=jnp.int32)[None, :]
    set_row = jnp.sum(jnp.where(item_hot, item_sets[0][None, :], 0), axis=1)
    set_hot = (
        set_row[:, None] == jnp.arange(action_mask.shape[0], dtype=jnp.int32)[None, :]
    ).astype(F32)
    mask_rows = jnp.dot(set_hot, action_mask.astype(F32))
    modality = tok_order // quarter_rows
    mod_hot = (
        modality[:, None] == jnp.arange(action_mask.shape[1], dtype=jnp.int32)[None, :]
    ).astype(F32)
    select = jnp.sum(mask_rows * mod_hot, axis=1)
    grad_down = (cotangent.astype(F32) * select[:, None]).astype(BF16)
    g_down_bias = jnp.sum(grad_down.astype(F32), axis=0)

    row = lambda v: v.astype(F32)[None, :]
    gain_one, shift_one = row(ln1_gain), row(ln1_bias)
    gain_two, shift_two = row(ln2_gain), row(ln2_bias)
    bias_qv = b_qv.astype(F32)
    bias_qkv = jnp.concatenate([bias_qv[0], jnp.zeros((width,), F32), bias_qv[1]])[None, :]
    b_col = jnp.broadcast_to(b_up.astype(F32)[:, None], (b_up.shape[0], 128))
    w_up_t = w_up.T
    w_down_t = w_down.T

    x, act_t, qkv = enter(order_col, arrived, gain_one, shift_one, w_qkv, bias_qkv)
    attn, lse = attend(qkv, tab, code_row, code_col)
    r, act2_t = middle(attn, x, w_out, row(b_out), gain_two, shift_two)
    sums = ()
    down_parts, up_parts, up_bias = [], [], []
    for part in range(FF_PARTS):
        y_t, g_t, g_down, g_up, g_bias = branch(
            part, act2_t, grad_down, w_up_t, w_down, w_up, w_down_t, b_col, sums
        )
        sums = (y_t, g_t)
        down_parts.append(links.all_sum(g_down, 0, 0))
        up_parts.append(links.all_sum(g_up, 0, 1))
        up_bias.append(g_bias[:, 0])
    mixed_out, gr, go, g_out, turn_sums = turn(
        y_t, g_t, r, grad_down, attn, w_out, row(b_down), gain_two
    )
    g_out = links.all_sum(g_out, 0, 0)
    first = links.small_sum(
        jnp.concatenate([turn_sums[:3].reshape(-1), g_down_bias, *up_bias]).reshape(-1, 128)
    ).reshape(-1)
    sums = ()
    qkv_parts, qv_parts = [], []
    for part in range(HEAD_PARTS):
        d, qv = attend_back(part, qkv, go, lse, tab, code_row, code_col)
        g_qkv, grad = project_back(part, act_t, d, w_qkv, sums)
        sums = (grad,)
        qkv_parts.append(links.all_sum(g_qkv, 1, part % 2))
        qv_parts.append(qv)
    back, leave_sums = leave(token_order, x, grad, gr, gain_one)
    token_grad = lax.all_to_all(back, AXES, split_axis=0, concat_axis=0, tiled=True)
    g_qv = jnp.concatenate(qv_parts, axis=1)
    last = links.small_sum(
        jnp.concatenate([leave_sums[:2].reshape(-1), g_qv.reshape(-1)]).reshape(-1, 128)
    ).reshape(-1)

    g_down = jnp.concatenate(down_parts, axis=0).astype(F32)
    g_up = jnp.concatenate(up_parts, axis=1).astype(F32)
    g_qkv = jnp.concatenate(
        [part[i] for i in range(3) for part in qkv_parts], axis=1
    ).astype(F32)
    pick = lambda v, i: v[i * width : (i + 1) * width]
    return (
        mixed_out,
        token_grad,
        pick(last, 0),
        pick(last, 1),
        g_qkv,
        last[2 * width :].reshape(2, width),
        g_out.astype(F32),
        pick(first, 2),
        pick(first, 0),
        pick(first, 1),
        g_up,
        first[4 * width :],
        g_down,
        pick(first, 3),
    )


def solution(mesh):
    split = P(AXES, None)
    in_specs = (split,) * 5 + (P(), split) + (P(),) * 12
    out_specs = (split, split) + (P(),) * 12
    return jax.shard_map(
        on_device, mesh=mesh, in_specs=in_specs, out_specs=out_specs, check_vma=False
    )
```

```python
import functools

import jax
import jax.numpy as jnp
from jax import lax
from jax.experimental import pallas as pl
from jax.experimental.pallas import tpu as pltpu
from jax.sharding import PartitionSpec as P


HEAD_DIM = 64
LN_EPS = 1e-05
NEG_BIG = -1e30
F32 = jnp.float32
BF16 = jnp.bfloat16
AXES = ("mod", "dp")
WINDOWS = (512, 640, 768, 1024)
Q_ROWS = 256
ROW_BLOCK = 256
FF_BLOCK = 256
HEAD_PARTS = 3
GELU_C = 0.7978845608028654
GELU_K = 0.044715


def dot_nn(left, right):
    return lax.dot_general(left, right, (((1,), (0,)), ((), ())), preferred_element_type=F32)


def dot_nt(left, right):
    return lax.dot_general(left, right, (((1,), (1,)), ((), ())), preferred_element_type=F32)


def cost(flops, moved, hard=0):
    return pl.CostEstimate(flops=flops, bytes_accessed=moved, transcendentals=hard)


def const_map(*_):
    return (0, 0)


def row_stats(values):
    mean = jnp.mean(values, axis=-1, keepdims=True)
    center = values - mean
    spread = jnp.mean(center * center, axis=-1, keepdims=True)
    return center, lax.rsqrt(spread + LN_EPS)


def norm_back(grad, hat, inv, gain):
    scaled = grad * gain
    return inv * (
        scaled
        - jnp.mean(scaled, axis=-1, keepdims=True)
        - hat * jnp.mean(scaled * hat, axis=-1, keepdims=True)
    )


def enter_kernel(order_ref, arr_ref, gain_ref, shift_ref, w_ref, bias_ref, x_ref, at_ref, qkv_ref):
    rows = arr_ref.shape[0]
    spots = lax.broadcasted_iota(jnp.int32, (order_ref.shape[0], rows), 1)
    hot = jnp.where(spots == order_ref[:, 0:1], 1.0, 0.0).astype(BF16)
    x = dot_nn(hot, arr_ref[...])
    x_ref[...] = x.astype(BF16)
    center, inv = row_stats(x)
    act = (center * inv * gain_ref[...] + shift_ref[...]).astype(BF16)
    at_ref[...] = act.T
    qkv_ref[...] = (dot_nn(act, w_ref[...]) + bias_ref[...]).astype(BF16)


def enter(order_col, arrived, gain, shift, w_qkv, bias):
    rows, width = arrived.shape
    triple = w_qkv.shape[1]
    blk = lambda i: (i, 0)
    return pl.pallas_call(
        enter_kernel,
        grid=(rows // ROW_BLOCK,),
        in_specs=[
            pl.BlockSpec((ROW_BLOCK, 128), blk),
            pl.BlockSpec((rows, width), const_map),
            pl.BlockSpec((1, width), const_map),
            pl.BlockSpec((1, width), const_map),
            pl.BlockSpec((width, triple), const_map),
            pl.BlockSpec((1, triple), const_map),
        ],
        out_specs=[
            pl.BlockSpec((ROW_BLOCK, width), blk),
            pl.BlockSpec((width, ROW_BLOCK), lambda i: (0, i)),
            pl.BlockSpec((ROW_BLOCK, triple), blk),
        ],
        out_shape=[
            jax.ShapeDtypeStruct((rows, width), BF16),
            jax.ShapeDtypeStruct((width, rows), BF16),
            jax.ShapeDtypeStruct((rows, triple), BF16),
        ],
        cost_estimate=cost(2 * rows * width * (triple + rows), 14 * rows * width),
        name="enter",
    )(order_col, arrived, gain, shift, w_qkv, bias)


def window_table(segment, rows):
    slots = jnp.arange(4, dtype=jnp.int32)
    starts = jnp.sum((segment[None, :] < slots[:, None]).astype(jnp.int32), axis=1)
    ends = jnp.sum((segment[None, :] <= slots[:, None]).astype(jnp.int32), axis=1)
    blocks = segment.reshape(rows // Q_ROWS, Q_ROWS)
    low = jnp.sum(jnp.where(blocks[:, :1] == slots[None, :], starts[None, :], 0), axis=1)
    high = jnp.sum(jnp.where(blocks[:, -1:] == slots[None, :], ends[None, :], 0), axis=1)
    start = (low // 128) * 128
    need = high - start
    wide = jnp.full_like(need, rows)
    for size in reversed(WINDOWS):
        wide = jnp.where(need <= size, size, wide)
    return jnp.stack([jnp.minimum(start, rows - wide), wide], axis=1).reshape(-1)


def lane_halves(block, scale=None):
    lane = lax.broadcasted_iota(jnp.int32, block.shape, 1)
    if scale is not None:
        block = block * jnp.asarray(scale, block.dtype)
    zero = jnp.zeros_like(block)
    return jnp.where(lane < HEAD_DIM, block, zero), jnp.where(lane < HEAD_DIM, zero, block)


def each_block(tab, rows, body):
    def block(b, carry):
        start, wide = tab[2 * b], tab[2 * b + 1]
        q_at = pl.multiple_of(b * Q_ROWS, Q_ROWS)
        k_at = pl.multiple_of(start, 128)
        for size in WINDOWS:
            pl.when(wide == size)(functools.partial(body, q_at, k_at, size))
        return carry

    lax.fori_loop(0, rows // Q_ROWS, block, 0)


def attend_kernel(tab, row_ref, col_ref, q_ref, k_ref, v_ref, o_ref, lse_ref, mask_ref):
    rows = q_ref.shape[0]

    @pl.when(pl.program_id(0) == 0)
    def _():
        key = row_ref[...]
        for r in range(0, rows, Q_ROWS):
            query = col_ref[r : r + Q_ROWS, 0:1]
            seen = (key <= query) & (key >= (query >> 1) * 2)
            mask_ref[r : r + Q_ROWS, :] = jnp.where(seen, 0.0, NEG_BIG)

    def one(q_at, k_at, size):
        halves = lane_halves(q_ref[pl.ds(q_at, Q_ROWS), :], HEAD_DIM**-0.5)
        keys = k_ref[pl.ds(k_at, size), :]
        vals = v_ref[pl.ds(k_at, size), :]
        outs, logs = [], []
        for half in halves:
            s = dot_nt(half, keys) + mask_ref[pl.ds(q_at, Q_ROWS), pl.ds(k_at, size)]
            top = jnp.max(s, axis=1, keepdims=True)
            e = jnp.exp(s - top)
            total = jnp.sum(e, axis=1, keepdims=True)
            outs.append(dot_nn(e.astype(BF16), vals) * (1.0 / total))
            logs.append(top + jnp.log(total))
        lane = lax.broadcasted_iota(jnp.int32, outs[0].shape, 1)
        o_ref[pl.ds(q_at, Q_ROWS), :] = jnp.where(lane < HEAD_DIM, outs[0], outs[1]).astype(BF16)
        stat = jnp.where(lane == 0, logs[0], logs[1])
        lse_ref[0, :, pl.ds(q_at, Q_ROWS)] = stat.T[0:2, :]

    each_block(tab, rows, one)


def attend(qkv, tab, code_row, code_col):
    rows = qkv.shape[0]
    width = qkv.shape[1] // 3
    pairs = width // 128
    return pl.pallas_call(
        attend_kernel,
        grid_spec=pltpu.PrefetchScalarGridSpec(
            num_scalar_prefetch=1,
            grid=(pairs,),
            in_specs=[
                pl.BlockSpec(code_row.shape, const_map),
                pl.BlockSpec(code_col.shape, const_map),
                pl.BlockSpec((rows, 128), lambda h, t: (0, h)),
                pl.BlockSpec((rows, 128), lambda h, t: (0, pairs + h)),
                pl.BlockSpec((rows, 128), lambda h, t: (0, 2 * pairs + h)),
            ],
            out_specs=[
                pl.BlockSpec((rows, 128), lambda h, t: (0, h)),
                pl.BlockSpec((1, 2, rows), lambda h, t: (h, 0, 0)),
            ],
            scratch_shapes=[pltpu.VMEM((rows, rows), F32)],
        ),
        out_shape=[
            jax.ShapeDtypeStruct((rows, width), BF16),
            jax.ShapeDtypeStruct((pairs, 2, rows), F32),
        ],
        cost_estimate=cost(16 * rows * rows * width, 8 * rows * width, 12 * rows * rows),
        name="attend",
    )(tab, code_row, code_col, qkv, qkv, qkv)


def attend_back_kernel(
    tab, row_ref, col_ref, q_ref, k_ref, v_ref, go_ref, lse_ref, g_ref, sum_ref, mask_ref, kt_ref, dk_ref, dv_ref
):
    rows = q_ref.shape[0]

    @pl.when(pl.program_id(0) == 0)
    def _():
        query = row_ref[...]
        low = (query >> 1) * 2
        for r in range(0, rows, Q_ROWS):
            key = col_ref[r : r + Q_ROWS, 0:1]
            seen = (key <= query) & (key >= low)
            mask_ref[r : r + Q_ROWS, :] = jnp.where(seen, 0.0, NEG_BIG)

    kt_ref[...] = k_ref[...].T
    dk_ref[...] = jnp.zeros_like(dk_ref)
    dv_ref[...] = jnp.zeros_like(dv_ref)

    def one(q_at, k_at, size):
        qs = pl.ds(q_at, Q_ROWS)
        ks = pl.ds(k_at, size)
        halves = lane_halves(q_ref[qs, :], HEAD_DIM**-0.5)
        grads = lane_halves(go_ref[qs, :])
        keys = k_ref[ks, :]
        vals = v_ref[ks, :]
        outs = []
        for h in range(2):
            s = dot_nt(keys, halves[h]) + mask_ref[ks, qs]
            p = jnp.exp(s - lse_ref[0, h : h + 1, qs])
            dp = dot_nt(vals, grads[h])
            delta = jnp.sum(p * dp, axis=0, keepdims=True)
            ds = (p * (dp - delta)).astype(BF16)
            dv_ref[ks, :] += dot_nn(p.astype(BF16), grads[h])
            dk_ref[ks, :] += dot_nn(ds, halves[h])
            outs.append(dot_nn(kt_ref[h * HEAD_DIM : (h + 1) * HEAD_DIM, ks], ds))
        dq = jnp.concatenate(outs, axis=0).T * HEAD_DIM**-0.5
        g_ref[0, qs, :] = dq.astype(BF16)

    each_block(tab, rows, one)
    g_ref[1] = dk_ref[...].astype(BF16)
    g_ref[2] = dv_ref[...].astype(BF16)
    sum_ref[0:1, :] = jnp.sum(g_ref[0].astype(F32), axis=0, keepdims=True)
    sum_ref[1:2, :] = jnp.sum(g_ref[2].astype(F32), axis=0, keepdims=True)


def attend_back(at, count, qkv, grad, lse, tab, code_row, code_col):
    rows = qkv.shape[0]
    width = qkv.shape[1] // 3
    pairs = width // 128
    share = count * 128
    return pl.pallas_call(
        attend_back_kernel,
        grid_spec=pltpu.PrefetchScalarGridSpec(
            num_scalar_prefetch=1,
            grid=(count,),
            in_specs=[
                pl.BlockSpec(code_row.shape, const_map),
                pl.BlockSpec(code_col.shape, const_map),
                pl.BlockSpec((rows, 128), lambda h, t: (0, at + h)),
                pl.BlockSpec((rows, 128), lambda h, t: (0, pairs + at + h)),
                pl.BlockSpec((rows, 128), lambda h, t: (0, 2 * pairs + at + h)),
                pl.BlockSpec((rows, 128), lambda h, t: (0, at + h)),
                pl.BlockSpec((1, 2, rows), lambda h, t: (at + h, 0, 0)),
            ],
            out_specs=[
                pl.BlockSpec((3, rows, 128), lambda h, t: (0, 0, h)),
                pl.BlockSpec((2, 128), lambda h, t: (0, h)),
            ],
            scratch_shapes=[
                pltpu.VMEM((rows, rows), F32),
                pltpu.VMEM((128, rows), BF16),
                pltpu.VMEM((rows, 128), F32),
                pltpu.VMEM((rows, 128), F32),
            ],
        ),
        out_shape=[
            jax.ShapeDtypeStruct((3, rows, share), BF16),
            jax.ShapeDtypeStruct((2, share), F32),
        ],
        cost_estimate=cost(40 * rows * rows * share, 14 * rows * share, 12 * rows * rows),
        name="attend_back",
    )(tab, code_row, code_col, qkv, qkv, qkv, grad, lse)


def middle_kernel(o_ref, x_ref, w_ref, b_ref, gain_ref, shift_ref, r_ref, at_ref):
    r = x_ref[...].astype(F32) + (dot_nn(o_ref[...], w_ref[...]) + b_ref[...])
    r_ref[...] = r
    center, inv = row_stats(r)
    at_ref[...] = (center * inv * gain_ref[...] + shift_ref[...]).astype(BF16).T


def middle(o, x, w_out, b_out, gain, shift):
    rows, width = x.shape
    blk = lambda i: (i, 0)
    vec = pl.BlockSpec((1, width), const_map)
    return pl.pallas_call(
        middle_kernel,
        grid=(rows // ROW_BLOCK,),
        in_specs=[
            pl.BlockSpec((ROW_BLOCK, width), blk),
            pl.BlockSpec((ROW_BLOCK, width), blk),
            pl.BlockSpec((width, width), const_map),
            vec,
            vec,
            vec,
        ],
        out_specs=[
            pl.BlockSpec((ROW_BLOCK, width), blk),
            pl.BlockSpec((width, ROW_BLOCK), lambda i: (0, i)),
        ],
        out_shape=[
            jax.ShapeDtypeStruct((rows, width), F32),
            jax.ShapeDtypeStruct((width, rows), BF16),
        ],
        cost_estimate=cost(2 * rows * width * width, 12 * rows * width),
        name="middle",
    )(o, x, w_out, b_out, gain, shift)


def branch_kernel(has_sum, half, at_ref, gd_ref, wut_ref, wd_ref, wu_ref, wdt_ref, bu_ref, *rest):
    if has_sum:
        y_in, g_in, y_ref, g_ref, gdown_ref, gup_ref, gb_ref = rest
    else:
        y_ref, g_ref, gdown_ref, gup_ref, gb_ref = rest

    @pl.when(pl.program_id(0) == 0)
    def _():
        if has_sum:
            y_ref[...] = y_in[...]
            g_ref[...] = g_in[...]
        else:
            y_ref[...] = jnp.zeros_like(y_ref)
            g_ref[...] = jnp.zeros_like(g_ref)

    act_t = at_ref[...]
    gd = gd_ref[...]
    u = dot_nn(wut_ref[...], act_t) + bu_ref[:, 0:1]
    square = u * u
    t = jnp.tanh(GELU_C * (u * (1.0 + GELU_K * square)))
    up = 0.5 * (1.0 + t)
    hidden = (u * up).astype(BF16)
    slope = up + (0.5 * GELU_C) * u * (1.0 - t * t) * (1.0 + (3.0 * GELU_K) * square)
    gu = (dot_nt(wd_ref[...], gd) * slope).astype(BF16)
    gdown_ref[...] = dot_nn(hidden, gd).astype(BF16)
    gup_ref[...] = dot_nt(act_t, gu).astype(BF16)
    y_ref[...] += dot_nn(wdt_ref[...], hidden)
    g_ref[...] += dot_nn(wu_ref[...], gu)
    total = jnp.sum(gu.astype(F32), axis=1, keepdims=True)
    gb_ref[...] = jnp.broadcast_to(total, (total.shape[0], 128)).T[0:8, :]


def branch(half, act_t, gd, w_up_t, w_down, w_up, w_down_t, b_col, sums):
    width, rows = act_t.shape
    share = w_down.shape[0] // 2
    steps = share // FF_BLOCK
    down = lambda c, half: (half[0] * steps + c, 0)
    across = lambda c, half: (0, half[0] * steps + c)
    whole = pl.BlockSpec((width, rows), const_map)
    return pl.pallas_call(
        functools.partial(branch_kernel, bool(sums)),
        grid_spec=pltpu.PrefetchScalarGridSpec(
            num_scalar_prefetch=1,
            grid=(steps,),
            in_specs=[
                whole,
                pl.BlockSpec((rows, width), const_map),
                pl.BlockSpec((FF_BLOCK, width), down),
                pl.BlockSpec((FF_BLOCK, width), down),
                pl.BlockSpec((width, FF_BLOCK), across),
                pl.BlockSpec((width, FF_BLOCK), across),
                pl.BlockSpec((FF_BLOCK, 128), down),
            ]
            + [whole] * len(sums),
            out_specs=[
                whole,
                whole,
                pl.BlockSpec((FF_BLOCK, width), lambda c, half: (c, 0)),
                pl.BlockSpec((width, FF_BLOCK), lambda c, half: (0, c)),
                pl.BlockSpec((8, FF_BLOCK), across),
            ],
        ),
        out_shape=[
            jax.ShapeDtypeStruct((width, rows), F32),
            jax.ShapeDtypeStruct((width, rows), F32),
            jax.ShapeDtypeStruct((share, width), BF16),
            jax.ShapeDtypeStruct((width, share), BF16),
            jax.ShapeDtypeStruct((8, 2 * share), F32),
        ],
        cost_estimate=cost(12 * rows * width * share, 20 * rows * width, rows * share),
        name="branch",
    )(half, act_t, gd, w_up_t, w_down, w_up, w_down_t, b_col, *sums)


def turn_kernel(yt_ref, gt_ref, r_ref, gd_ref, o_ref, w_ref, b_ref, gain_ref, mix_ref, gr_ref, go_ref, gw_ref, sum_ref, acc_ref):
    step = pl.program_id(0)

    @pl.when(step == 0)
    def _():
        acc_ref[...] = jnp.zeros_like(acc_ref)
        sum_ref[...] = jnp.zeros_like(sum_ref)

    r = r_ref[...]
    mix_ref[...] = (r + (yt_ref[...].T + b_ref[...])).astype(BF16)
    grad = gt_ref[...].T
    center, inv = row_stats(r)
    hat = center * inv
    gr = gd_ref[...].astype(F32) + norm_back(grad, hat, inv, gain_ref[...])
    gr_ref[...] = gr
    ga = gr.astype(BF16)
    go_ref[...] = dot_nt(ga, w_ref[...]).astype(BF16)
    acc_ref[...] += dot_nn(o_ref[...].T, ga)
    sum_ref[0:1, :] += jnp.sum(grad * hat, axis=0, keepdims=True)
    sum_ref[1:2, :] += jnp.sum(grad, axis=0, keepdims=True)
    sum_ref[2:3, :] += jnp.sum(ga.astype(F32), axis=0, keepdims=True)

    @pl.when(step == pl.num_programs(0) - 1)
    def _():
        gw_ref[...] = acc_ref[...].astype(BF16)


def turn(y_t, g_t, r, gd, o, w_out, b_down, gain):
    rows, width = r.shape
    blk = lambda i: (i, 0)
    across = lambda i: (0, i)
    row_spec = pl.BlockSpec((ROW_BLOCK, width), blk)
    vec = pl.BlockSpec((1, width), const_map)
    return pl.pallas_call(
        turn_kernel,
        grid=(rows // ROW_BLOCK,),
        in_specs=[
            pl.BlockSpec((width, ROW_BLOCK), across),
            pl.BlockSpec((width, ROW_BLOCK), across),
            row_spec,
            row_spec,
            row_spec,
            pl.BlockSpec((width, width), const_map),
            vec,
            vec,
        ],
        out_specs=[
            row_spec,
            row_spec,
            row_spec,
            pl.BlockSpec((width, width), const_map),
            pl.BlockSpec((8, width), const_map),
        ],
        out_shape=[
            jax.ShapeDtypeStruct((rows, width), BF16),
            jax.ShapeDtypeStruct((rows, width), F32),
            jax.ShapeDtypeStruct((rows, width), BF16),
            jax.ShapeDtypeStruct((width, width), BF16),
            jax.ShapeDtypeStruct((8, width), F32),
        ],
        scratch_shapes=[pltpu.VMEM((width, width), F32)],
        cost_estimate=cost(4 * rows * width * width, 24 * rows * width),
        name="turn",
    )(y_t, g_t, r, gd, o, w_out, b_down, gain)


def project_back_kernel(has_sum, count, at_ref, *refs):
    d_refs, w_ref = refs[:count], refs[count]
    gw_ref, g_ref = refs[-2:]
    d = jnp.concatenate([ref[0] for ref in d_refs], axis=1) if count > 1 else d_refs[0][0]
    gw_ref[...] = dot_nn(at_ref[...], d).astype(BF16)
    term = dot_nt(d, w_ref[...])

    @pl.when(pl.program_id(0) == 0)
    def _():
        g_ref[...] = refs[count + 1][...] + term if has_sum else term

    @pl.when(pl.program_id(0) > 0)
    def _():
        g_ref[...] += term


def project_back(part, act_t, ds, w_qkv, sums):
    width, rows = act_t.shape
    share = sum(d.shape[2] for d in ds)
    whole = pl.BlockSpec((rows, width), const_map)
    return pl.pallas_call(
        functools.partial(project_back_kernel, bool(sums), len(ds)),
        grid=(3,),
        in_specs=[pl.BlockSpec((width, rows), const_map)]
        + [pl.BlockSpec((1, rows, d.shape[2]), lambda i: (i, 0, 0)) for d in ds]
        + [pl.BlockSpec((width, share), lambda i: (0, HEAD_PARTS * i + part))]
        + [whole] * len(sums),
        out_specs=[pl.BlockSpec((width, share), lambda i: (0, i)), whole],
        out_shape=[
            jax.ShapeDtypeStruct((width, 3 * share), BF16),
            jax.ShapeDtypeStruct((rows, width), F32),
        ],
        cost_estimate=cost(12 * rows * width * share, 12 * rows * width),
        name="project_back",
    )(act_t, *ds, w_qkv, *sums)


def leave_kernel(
    mine, order_ref, x_ref, g_ref, gr_ref, gain_ref, turn_ref, down_ref, up0_ref, up1_ref, *rest
):
    qv_refs = rest[:-3]
    back_ref, sum_ref, gx_ref = rest[-3:]
    step = pl.program_id(0)
    rows, width = back_ref.shape

    @pl.when(step == 0)
    def _():
        sum_ref[...] = jnp.zeros_like(sum_ref)
        at = 0
        for ref in qv_refs:
            sum_ref[2:4, at : at + ref.shape[1]] = ref[...]
            at += ref.shape[1]
        sum_ref[4:7, :] = turn_ref[0:3, :]
        sum_ref[7:8, :] = down_ref[...]
        pieces = up0_ref.shape[1] // width
        for n in range(pieces):
            cut = slice(n * width, (n + 1) * width)
            kept = mine[0] == (2 * n) // pieces
            sum_ref[8 + n : 9 + n, :] = jnp.where(kept, up1_ref[0:1, cut], up0_ref[0:1, cut])

    grad = g_ref[...]
    center, inv = row_stats(x_ref[...].astype(F32))
    hat = center * inv
    gx = gr_ref[...] + norm_back(grad, hat, inv, gain_ref[...])
    gx_ref[pl.ds(pl.multiple_of(step * ROW_BLOCK, ROW_BLOCK), ROW_BLOCK), :] = gx.astype(BF16)
    sum_ref[0:1, :] += jnp.sum(grad * hat, axis=0, keepdims=True)
    sum_ref[1:2, :] += jnp.sum(grad, axis=0, keepdims=True)

    @pl.when(step == pl.num_programs(0) - 1)
    def _():
        for r in range(0, rows, ROW_BLOCK):
            spots = lax.broadcasted_iota(jnp.int32, (ROW_BLOCK, rows), 0) + r
            hot = jnp.where(spots == order_ref[...], 1.0, 0.0).astype(BF16)
            back_ref[r : r + ROW_BLOCK, :] = dot_nn(hot, gx_ref[...]).astype(BF16)


def leave(mine, order_row, x, grad, gr, gain, turn_sums, down_bias, up_biases, qvs):
    rows, width = x.shape
    row_spec = pl.BlockSpec((ROW_BLOCK, width), lambda i, m: (i, 0))
    full = lambda v: pl.BlockSpec(v.shape, const_map)
    smalls = (turn_sums, down_bias, *up_biases, *qvs)
    lines = 8 + up_biases[0].shape[1] // width
    lines += -lines % 8
    return pl.pallas_call(
        leave_kernel,
        grid_spec=pltpu.PrefetchScalarGridSpec(
            num_scalar_prefetch=1,
            grid=(rows // ROW_BLOCK,),
            in_specs=[full(order_row), row_spec, row_spec, row_spec, full(gain)]
            + [full(v) for v in smalls],
            out_specs=[
                pl.BlockSpec((rows, width), const_map),
                pl.BlockSpec((lines, width), const_map),
            ],
            scratch_shapes=[pltpu.VMEM((rows, width), BF16)],
        ),
        out_shape=[
            jax.ShapeDtypeStruct((rows, width), BF16),
            jax.ShapeDtypeStruct((lines, width), F32),
        ],
        cost_estimate=cost(2 * rows * rows * width, 12 * rows * width),
        name="leave",
    )(mine, order_row, x, grad, gr, gain, *smalls)


def finish_branch_kernel(bits, down0_ref, down1_ref, up0_ref, up1_ref, down_ref, up_ref):
    mine = pl.program_id(0) == bits[0]

    @pl.when(mine)
    def _():
        down_ref[...] = down0_ref[...].astype(F32)
        up_ref[...] = up0_ref[...].astype(F32)

    @pl.when(jnp.logical_not(mine))
    def _():
        down_ref[...] = down1_ref[...].astype(F32)
        up_ref[...] = up1_ref[...].astype(F32)


def finish_branch(bits, downs, ups):
    share, width = downs[0].shape
    steps = 4
    own = lambda h, i, bits: jnp.where(h == bits[0], i, jnp.where(h == 0, 0, steps - 1))
    far = lambda h, i, bits: jnp.where(h != bits[0], i, jnp.where(h == 0, 0, steps - 1))
    row = lambda pick: pl.BlockSpec((share // steps, width), lambda h, i, b: (pick(h, i, b), 0))
    col = lambda pick: pl.BlockSpec((width // steps, share), lambda h, i, b: (pick(h, i, b), 0))
    return pl.pallas_call(
        finish_branch_kernel,
        grid_spec=pltpu.PrefetchScalarGridSpec(
            num_scalar_prefetch=1,
            grid=(2, steps),
            in_specs=[row(own), row(far), col(own), col(far)],
            out_specs=[
                pl.BlockSpec((share // steps, width), lambda h, i, b: (h * steps + i, 0)),
                pl.BlockSpec((width // steps, share), lambda h, i, b: (i, h)),
            ],
        ),
        out_shape=[
            jax.ShapeDtypeStruct((2 * share, width), F32),
            jax.ShapeDtypeStruct((width, 2 * share), F32),
        ],
        cost_estimate=cost(share * width, 12 * share * width),
        name="finish_branch",
    )(bits, *downs, *ups)


def finish_project_kernel(bits, early0_ref, early1_ref, late0_ref, late1_ref, out_ref, qkv_ref):
    share = out_ref.shape[1] // HEAD_PARTS

    def put(early, late):
        out_ref[...] = early[0].astype(F32)
        for p, part in enumerate((early[1], late[0], late[1])):
            for i in range(3):
                at = (i * HEAD_PARTS + p) * share
                qkv_ref[:, at : at + share] = part[:, i * share : (i + 1) * share].astype(F32)

    mine = pl.program_id(0) == bits[0]
    pl.when(mine)(lambda: put(early0_ref, late0_ref))
    pl.when(jnp.logical_not(mine))(lambda: put(early1_ref, late1_ref))


def finish_project(bits, earlies, lates):
    _, half, width = earlies[0].shape
    steps = 3
    own = lambda h, i, b: (0, jnp.where(h == b[0], i, jnp.where(h == 0, 0, steps - 1)), 0)
    far = lambda h, i, b: (0, jnp.where(h != b[0], i, jnp.where(h == 0, 0, steps - 1)), 0)
    blk = (2, half // steps, width)
    out = lambda h, i, b: (h * steps + i, 0)
    return pl.pallas_call(
        finish_project_kernel,
        grid_spec=pltpu.PrefetchScalarGridSpec(
            num_scalar_prefetch=1,
            grid=(2, steps),
            in_specs=[
                pl.BlockSpec(blk, own),
                pl.BlockSpec(blk, far),
                pl.BlockSpec(blk, own),
                pl.BlockSpec(blk, far),
            ],
            out_specs=[
                pl.BlockSpec((half // steps, width), out),
                pl.BlockSpec((half // steps, 3 * width), out),
            ],
        ),
        out_shape=[
            jax.ShapeDtypeStruct((2 * half, width), F32),
            jax.ShapeDtypeStruct((2 * half, 3 * width), F32),
        ],
        cost_estimate=cost(width * width, 24 * width * width),
        name="finish_project",
    )(bits, *earlies, *lates)


class Links:
    def __init__(self):
        inner = lax.axis_size("dp")
        self.total = lax.axis_size("mod") * inner
        me = lax.axis_index("mod") * inner + lax.axis_index("dp")
        width = self.total.bit_length() - 1
        self.bits = (me >> jnp.arange(width, dtype=jnp.int32)) & 1
        self.me = me
        low = range(1, inner.bit_length() - 1)
        high = range(inner.bit_length() - 1, width)
        self.orders = ([0, *high, *low], [0, *reversed(high), *low])

    def swap(self, value, bit):
        pairs = [(i, i ^ (1 << bit)) for i in range(self.total)]
        return lax.ppermute(value, AXES, pairs)

    def side(self, bit):
        return (self.me >> bit) & 1

    def half(self, value, axis, which):
        shape = value.shape
        cut = shape[:axis] + (2, shape[axis] // 2) + shape[axis + 1 :]
        return lax.dynamic_index_in_dim(value.reshape(cut), which, axis, keepdims=False)

    def scatter_sum(self, value, axis, order, first=0):
        for stage in range(first, len(order)):
            bit = order[stage]
            mine = self.side(bit)
            send = self.half(value, axis, 1 - mine).astype(BF16)
            keep = self.half(value, axis, mine).astype(F32)
            got = self.swap(send, bit)
            value = keep + got.astype(F32)
        return value.astype(BF16)

    def join(self, value, other, axis, bit):
        shape = value.shape
        side = lax.broadcasted_iota(jnp.int32, shape[:axis] + (2,) + shape[axis:], axis)
        both = jnp.where(
            side == self.side(bit), jnp.expand_dims(value, axis), jnp.expand_dims(other, axis)
        )
        return both.reshape(shape[:axis] + (2 * shape[axis],) + shape[axis + 1 :])

    def gather(self, values, axis, small=None):
        if small is not None:
            small = small + self.swap(small, self.orders[0][0])
        for stage in reversed(range(len(self.orders[0]))):
            if small is not None and stage:
                *values, small = lax.optimization_barrier((*values, small))
                small = small + self.swap(small, self.orders[0][stage])
            others = [self.swap(v, order[stage]) for v, order in zip(values, self.orders)]
            pairs = list(zip(values, others))
            if stage:
                values = [
                    self.join(v, w, axis, o[stage]) for (v, w), o in zip(pairs, self.orders)
                ]
        return pairs if small is None else (*pairs, small)


def on_device(
    tokens,
    token_order,
    item_ids,
    step_blocks,
    item_sets,
    action_mask,
    cotangent,
    ln1_gain,
    ln1_bias,
    w_qkv,
    b_qv,
    w_out,
    b_out,
    ln2_gain,
    ln2_bias,
    w_up,
    b_up,
    w_down,
    b_down,
):
    rows, width = tokens.shape
    quarter_rows = rows // lax.axis_size("mod")
    links = Links()
    arrived = lax.all_to_all(tokens, AXES, split_axis=0, concat_axis=0, tiled=True)

    tok_order = token_order[0]
    segment = item_ids[0]
    code = segment * 2 + step_blocks[0]
    code_row = code[None, :]
    code_col = jnp.broadcast_to(code[:, None], (rows, 128))
    order_col = jnp.broadcast_to(tok_order[:, None], (rows, 128))
    tab = window_table(segment, rows)
    item_hot = segment[:, None] == jnp.arange(item_sets.shape[1], dtype=jnp.int32)[None, :]
    set_row = jnp.sum(jnp.where(item_hot, item_sets[0][None, :], 0), axis=1)
    set_hot = (
        set_row[:, None] == jnp.arange(action_mask.shape[0], dtype=jnp.int32)[None, :]
    ).astype(F32)
    mask_rows = jnp.dot(set_hot, action_mask.astype(F32))
    modality = tok_order // quarter_rows
    mod_hot = (
        modality[:, None] == jnp.arange(action_mask.shape[1], dtype=jnp.int32)[None, :]
    ).astype(F32)
    select = jnp.sum(mask_rows * mod_hot, axis=1)
    grad_down = (cotangent.astype(F32) * select[:, None]).astype(BF16)
    g_down_bias = jnp.sum(grad_down.astype(F32), axis=0)[None, :]

    row = lambda v: v.astype(F32)[None, :]
    gain_one, shift_one = row(ln1_gain), row(ln1_bias)
    gain_two, shift_two = row(ln2_gain), row(ln2_bias)
    bias_qv = b_qv.astype(F32)
    bias_qkv = jnp.concatenate([bias_qv[0], jnp.zeros((width,), F32), bias_qv[1]])[None, :]
    b_col = jnp.broadcast_to(b_up.astype(F32)[:, None], (b_up.shape[0], 128))
    w_up_t = w_up.T
    w_down_t = w_down.T

    x, act_t, qkv = enter(order_col, arrived, gain_one, shift_one, w_qkv, bias_qkv)
    attn, lse = attend(qkv, tab, code_row, code_col)
    r, act2_t = middle(attn, x, w_out, row(b_out), gain_two, shift_two)
    bits = links.bits
    mine = bits[0:1]
    sums, halves, biases = (), [], []
    for half in (1 - mine, mine):
        y_t, g_t, g_down, g_up, g_bias = branch(
            half, act2_t, grad_down, w_up_t, w_down, w_up, w_down_t, b_col, sums
        )
        sums = (y_t, g_t)
        halves.append((g_down, g_up))
        biases.append(g_bias)
    parts = []
    for sent, kept, order in zip(halves[0], halves[1], links.orders):
        got = links.swap(sent, 0)
        parts.append(links.scatter_sum(kept.astype(F32) + got.astype(F32), 0, order, 1))
    downs, ups = links.gather(parts, 0)
    g_down, g_up = finish_branch(bits, downs, ups)
    mixed_out, gr, go, g_out, turn_sums = turn(
        y_t, g_t, r, grad_down, attn, w_out, row(b_down), gain_two
    )
    sums = ()
    units, qv_parts = [g_out], []
    for part, runs in enumerate(((2,), (2,), (1, 1))):
        ds, at = [], 2 * part
        for count in runs:
            d, qv = attend_back(at, count, qkv, go, lse, tab, code_row, code_col)
            at += count
            ds.append(d)
            qv_parts.append(qv)
        g_qkv, grad = project_back(part, act_t, ds, w_qkv, sums)
        sums = (grad,)
        units.append(g_qkv)
    early = links.scatter_sum(jnp.stack(units[:2]), 1, links.orders[0])
    late = links.scatter_sum(jnp.stack(units[2:]), 1, links.orders[1])
    back, small = leave(
        mine, token_order, x, grad, gr, gain_one, turn_sums, g_down_bias, biases, qv_parts
    )
    token_grad = lax.all_to_all(back, AXES, split_axis=0, concat_axis=0, tiled=True)
    earlies, lates, small = links.gather((early, late), 1, small)
    g_out, g_qkv = finish_project(bits, earlies, lates)
    lines = b_up.shape[0] // width
    return (
        mixed_out,
        token_grad,
        small[0],
        small[1],
        g_qkv,
        small[2:4],
        g_out,
        small[6],
        small[4],
        small[5],
        g_up,
        small[8 : 8 + lines].reshape(-1),
        g_down,
        small[7],
    )


def solution(mesh):
    split = P(AXES, None)
    in_specs = (split,) * 5 + (P(), split) + (P(),) * 12
    out_specs = (split, split) + (P(),) * 12

    return jax.shard_map(
        on_device, mesh=mesh, in_specs=in_specs, out_specs=out_specs, check_vma=False
    )
```

```python
import functools

import jax
import jax.numpy as jnp
from jax import lax
from jax.experimental import pallas as pl
from jax.experimental.pallas import tpu as pltpu
from jax.sharding import PartitionSpec as P


HEAD_DIM = 64
LN_EPS = 1e-05
NEG_BIG = -1e30
F32 = jnp.float32
BF16 = jnp.bfloat16
AXES = ("mod", "dp")
WINDOWS = (512, 640, 768, 1024)
Q_ROWS = 256
ROW_BLOCK = 256
FF_BLOCK = 256
HEAD_PARTS = 3
GELU_C = 0.7978845608028654
GELU_K = 0.044715


def dot_nn(left, right):
    return lax.dot_general(left, right, (((1,), (0,)), ((), ())), preferred_element_type=F32)


def dot_nt(left, right):
    return lax.dot_general(left, right, (((1,), (1,)), ((), ())), preferred_element_type=F32)


def cost(flops, moved, hard=0):
    return pl.CostEstimate(flops=flops, bytes_accessed=moved, transcendentals=hard)


def const_map(*_):
    return (0, 0)


def row_stats(values):
    mean = jnp.mean(values, axis=-1, keepdims=True)
    center = values - mean
    spread = jnp.mean(center * center, axis=-1, keepdims=True)
    return center, lax.rsqrt(spread + LN_EPS)


def norm_back(grad, hat, inv, gain):
    scaled = grad * gain
    return inv * (
        scaled
        - jnp.mean(scaled, axis=-1, keepdims=True)
        - hat * jnp.mean(scaled * hat, axis=-1, keepdims=True)
    )


def enter_kernel(order_ref, arr_ref, gain_ref, shift_ref, w_ref, bias_ref, x_ref, at_ref, qkv_ref):
    rows = arr_ref.shape[0]
    spots = lax.broadcasted_iota(jnp.int32, (order_ref.shape[0], rows), 1)
    hot = jnp.where(spots == order_ref[:, 0:1], 1.0, 0.0).astype(BF16)
    x = dot_nn(hot, arr_ref[...])
    x_ref[...] = x.astype(BF16)
    center, inv = row_stats(x)
    act = (center * inv * gain_ref[...] + shift_ref[...]).astype(BF16)
    at_ref[...] = act.T
    qkv_ref[...] = (dot_nn(act, w_ref[...]) + bias_ref[...]).astype(BF16)


def enter(order_col, arrived, gain, shift, w_qkv, bias):
    rows, width = arrived.shape
    triple = w_qkv.shape[1]
    blk = lambda i: (i, 0)
    return pl.pallas_call(
        enter_kernel,
        grid=(rows // ROW_BLOCK,),
        in_specs=[
            pl.BlockSpec((ROW_BLOCK, 128), blk),
            pl.BlockSpec((rows, width), const_map),
            pl.BlockSpec((1, width), const_map),
            pl.BlockSpec((1, width), const_map),
            pl.BlockSpec((width, triple), const_map),
            pl.BlockSpec((1, triple), const_map),
        ],
        out_specs=[
            pl.BlockSpec((ROW_BLOCK, width), blk),
            pl.BlockSpec((width, ROW_BLOCK), lambda i: (0, i)),
            pl.BlockSpec((ROW_BLOCK, triple), blk),
        ],
        out_shape=[
            jax.ShapeDtypeStruct((rows, width), BF16),
            jax.ShapeDtypeStruct((width, rows), BF16),
            jax.ShapeDtypeStruct((rows, triple), BF16),
        ],
        cost_estimate=cost(2 * rows * width * (triple + rows), 14 * rows * width),
        name="enter",
    )(order_col, arrived, gain, shift, w_qkv, bias)


def window_table(segment, rows):
    slots = jnp.arange(4, dtype=jnp.int32)
    starts = jnp.sum((segment[None, :] < slots[:, None]).astype(jnp.int32), axis=1)
    ends = jnp.sum((segment[None, :] <= slots[:, None]).astype(jnp.int32), axis=1)
    blocks = segment.reshape(rows // Q_ROWS, Q_ROWS)
    low = jnp.sum(jnp.where(blocks[:, :1] == slots[None, :], starts[None, :], 0), axis=1)
    high = jnp.sum(jnp.where(blocks[:, -1:] == slots[None, :], ends[None, :], 0), axis=1)
    start = (low // 128) * 128
    need = high - start
    wide = jnp.full_like(need, rows)
    for size in reversed(WINDOWS):
        wide = jnp.where(need <= size, size, wide)
    return jnp.stack([jnp.minimum(start, rows - wide), wide], axis=1).reshape(-1)


def lane_halves(block, scale=None):
    lane = lax.broadcasted_iota(jnp.int32, block.shape, 1)
    if scale is not None:
        block = block * jnp.asarray(scale, block.dtype)
    zero = jnp.zeros_like(block)
    return jnp.where(lane < HEAD_DIM, block, zero), jnp.where(lane < HEAD_DIM, zero, block)


def each_block(tab, rows, body):
    def block(b, carry):
        start, wide = tab[2 * b], tab[2 * b + 1]
        q_at = pl.multiple_of(b * Q_ROWS, Q_ROWS)
        k_at = pl.multiple_of(start, 128)
        for size in WINDOWS:
            pl.when(wide == size)(functools.partial(body, q_at, k_at, size))
        return carry

    lax.fori_loop(0, rows // Q_ROWS, block, 0)


def attend_kernel(tab, row_ref, col_ref, q_ref, k_ref, v_ref, o_ref, lse_ref, mask_ref):
    rows = q_ref.shape[0]

    @pl.when(pl.program_id(0) == 0)
    def _():
        key = row_ref[...]
        for r in range(0, rows, Q_ROWS):
            query = col_ref[r : r + Q_ROWS, 0:1]
            seen = (key <= query) & (key >= (query >> 1) * 2)
            mask_ref[r : r + Q_ROWS, :] = jnp.where(seen, 0.0, NEG_BIG)

    def one(q_at, k_at, size):
        halves = lane_halves(q_ref[pl.ds(q_at, Q_ROWS), :], HEAD_DIM**-0.5)
        keys = k_ref[pl.ds(k_at, size), :]
        vals = v_ref[pl.ds(k_at, size), :]
        outs, logs = [], []
        for half in halves:
            s = dot_nt(half, keys) + mask_ref[pl.ds(q_at, Q_ROWS), pl.ds(k_at, size)]
            top = jnp.max(s, axis=1, keepdims=True)
            e = jnp.exp(s - top)
            total = jnp.sum(e, axis=1, keepdims=True)
            outs.append(dot_nn(e.astype(BF16), vals) * (1.0 / total))
            logs.append(top + jnp.log(total))
        lane = lax.broadcasted_iota(jnp.int32, outs[0].shape, 1)
        o_ref[pl.ds(q_at, Q_ROWS), :] = jnp.where(lane < HEAD_DIM, outs[0], outs[1]).astype(BF16)
        stat = jnp.where(lane == 0, logs[0], logs[1])
        lse_ref[0, :, pl.ds(q_at, Q_ROWS)] = stat.T[0:2, :]

    each_block(tab, rows, one)


def attend(qkv, tab, code_row, code_col):
    rows = qkv.shape[0]
    width = qkv.shape[1] // 3
    pairs = width // 128
    return pl.pallas_call(
        attend_kernel,
        grid_spec=pltpu.PrefetchScalarGridSpec(
            num_scalar_prefetch=1,
            grid=(pairs,),
            in_specs=[
                pl.BlockSpec(code_row.shape, const_map),
                pl.BlockSpec(code_col.shape, const_map),
                pl.BlockSpec((rows, 128), lambda h, t: (0, h)),
                pl.BlockSpec((rows, 128), lambda h, t: (0, pairs + h)),
                pl.BlockSpec((rows, 128), lambda h, t: (0, 2 * pairs + h)),
            ],
            out_specs=[
                pl.BlockSpec((rows, 128), lambda h, t: (0, h)),
                pl.BlockSpec((1, 2, rows), lambda h, t: (h, 0, 0)),
            ],
            scratch_shapes=[pltpu.VMEM((rows, rows), F32)],
        ),
        out_shape=[
            jax.ShapeDtypeStruct((rows, width), BF16),
            jax.ShapeDtypeStruct((pairs, 2, rows), F32),
        ],
        cost_estimate=cost(16 * rows * rows * width, 8 * rows * width, 12 * rows * rows),
        name="attend",
    )(tab, code_row, code_col, qkv, qkv, qkv)


def attend_back_kernel(
    tab, row_ref, col_ref, q_ref, k_ref, v_ref, go_ref, lse_ref, g_ref, sum_ref, mask_ref, kt_ref, dk_ref, dv_ref
):
    rows = q_ref.shape[0]

    @pl.when(pl.program_id(0) == 0)
    def _():
        query = row_ref[...]
        low = (query >> 1) * 2
        for r in range(0, rows, Q_ROWS):
            key = col_ref[r : r + Q_ROWS, 0:1]
            seen = (key <= query) & (key >= low)
            mask_ref[r : r + Q_ROWS, :] = jnp.where(seen, 0.0, NEG_BIG)

    kt_ref[...] = k_ref[...].T
    dk_ref[...] = jnp.zeros_like(dk_ref)
    dv_ref[...] = jnp.zeros_like(dv_ref)

    def one(q_at, k_at, size):
        qs = pl.ds(q_at, Q_ROWS)
        ks = pl.ds(k_at, size)
        halves = lane_halves(q_ref[qs, :], HEAD_DIM**-0.5)
        grads = lane_halves(go_ref[qs, :])
        keys = k_ref[ks, :]
        vals = v_ref[ks, :]
        outs = []
        for h in range(2):
            s = dot_nt(keys, halves[h]) + mask_ref[ks, qs]
            p = jnp.exp(s - lse_ref[0, h : h + 1, qs])
            dp = dot_nt(vals, grads[h])
            delta = jnp.sum(p * dp, axis=0, keepdims=True)
            ds = (p * (dp - delta)).astype(BF16)
            dv_ref[ks, :] += dot_nn(p.astype(BF16), grads[h])
            dk_ref[ks, :] += dot_nn(ds, halves[h])
            outs.append(dot_nn(kt_ref[h * HEAD_DIM : (h + 1) * HEAD_DIM, ks], ds))
        dq = jnp.concatenate(outs, axis=0).T * HEAD_DIM**-0.5
        g_ref[0, qs, :] = dq.astype(BF16)

    each_block(tab, rows, one)
    g_ref[1] = dk_ref[...].astype(BF16)
    g_ref[2] = dv_ref[...].astype(BF16)
    sum_ref[0:1, :] = jnp.sum(g_ref[0].astype(F32), axis=0, keepdims=True)
    sum_ref[1:2, :] = jnp.sum(g_ref[2].astype(F32), axis=0, keepdims=True)


def attend_back(at, count, qkv, grad, lse, tab, code_row, code_col):
    rows = qkv.shape[0]
    width = qkv.shape[1] // 3
    pairs = width // 128
    share = count * 128
    return pl.pallas_call(
        attend_back_kernel,
        grid_spec=pltpu.PrefetchScalarGridSpec(
            num_scalar_prefetch=1,
            grid=(count,),
            in_specs=[
                pl.BlockSpec(code_row.shape, const_map),
                pl.BlockSpec(code_col.shape, const_map),
                pl.BlockSpec((rows, 128), lambda h, t: (0, at + h)),
                pl.BlockSpec((rows, 128), lambda h, t: (0, pairs + at + h)),
                pl.BlockSpec((rows, 128), lambda h, t: (0, 2 * pairs + at + h)),
                pl.BlockSpec((rows, 128), lambda h, t: (0, at + h)),
                pl.BlockSpec((1, 2, rows), lambda h, t: (at + h, 0, 0)),
            ],
            out_specs=[
                pl.BlockSpec((3, rows, 128), lambda h, t: (0, 0, h)),
                pl.BlockSpec((2, 128), lambda h, t: (0, h)),
            ],
            scratch_shapes=[
                pltpu.VMEM((rows, rows), F32),
                pltpu.VMEM((128, rows), BF16),
                pltpu.VMEM((rows, 128), F32),
                pltpu.VMEM((rows, 128), F32),
            ],
        ),
        out_shape=[
            jax.ShapeDtypeStruct((3, rows, share), BF16),
            jax.ShapeDtypeStruct((2, share), F32),
        ],
        cost_estimate=cost(40 * rows * rows * share, 14 * rows * share, 12 * rows * rows),
        name="attend_back",
    )(tab, code_row, code_col, qkv, qkv, qkv, grad, lse)


def middle_kernel(o_ref, x_ref, w_ref, b_ref, gain_ref, shift_ref, r_ref, a_ref, at_ref):
    r = x_ref[...].astype(F32) + (dot_nn(o_ref[...], w_ref[...]) + b_ref[...])
    r_ref[...] = r
    center, inv = row_stats(r)
    act = (center * inv * gain_ref[...] + shift_ref[...]).astype(BF16)
    a_ref[...] = act
    at_ref[...] = act.T


def middle(o, x, w_out, b_out, gain, shift):
    rows, width = x.shape
    blk = lambda i: (i, 0)
    vec = pl.BlockSpec((1, width), const_map)
    return pl.pallas_call(
        middle_kernel,
        grid=(rows // ROW_BLOCK,),
        in_specs=[
            pl.BlockSpec((ROW_BLOCK, width), blk),
            pl.BlockSpec((ROW_BLOCK, width), blk),
            pl.BlockSpec((width, width), const_map),
            vec,
            vec,
            vec,
        ],
        out_specs=[
            pl.BlockSpec((ROW_BLOCK, width), blk),
            pl.BlockSpec((ROW_BLOCK, width), blk),
            pl.BlockSpec((width, ROW_BLOCK), lambda i: (0, i)),
        ],
        out_shape=[
            jax.ShapeDtypeStruct((rows, width), F32),
            jax.ShapeDtypeStruct((rows, width), BF16),
            jax.ShapeDtypeStruct((width, rows), BF16),
        ],
        cost_estimate=cost(2 * rows * width * width, 12 * rows * width),
        name="middle",
    )(o, x, w_out, b_out, gain, shift)


def branch_kernel(has_sum, half, at_ref, a_ref, gd_ref, wut_ref, wd_ref, wu_ref, wdt_ref, bu_ref, *rest):
    if has_sum:
        y_in, g_in, y_ref, g_ref, gw_ref, gb_ref = rest
    else:
        y_ref, g_ref, gw_ref, gb_ref = rest

    @pl.when(pl.program_id(0) == 0)
    def _():
        if has_sum:
            y_ref[...] = y_in[...]
            g_ref[...] = g_in[...]
        else:
            y_ref[...] = jnp.zeros_like(y_ref)
            g_ref[...] = jnp.zeros_like(g_ref)

    act_t = at_ref[...]
    gd = gd_ref[...]
    u = dot_nn(wut_ref[...], act_t) + bu_ref[:, 0:1]
    square = u * u
    t = jnp.tanh(GELU_C * (u * (1.0 + GELU_K * square)))
    up = 0.5 * (1.0 + t)
    hidden = (u * up).astype(BF16)
    slope = up + (0.5 * GELU_C) * u * (1.0 - t * t) * (1.0 + (3.0 * GELU_K) * square)
    gu = (dot_nt(wd_ref[...], gd) * slope).astype(BF16)
    gw_ref[0] = dot_nn(hidden, gd).astype(BF16)
    gw_ref[1] = dot_nn(gu, a_ref[...]).astype(BF16)
    y_ref[...] += dot_nn(wdt_ref[...], hidden)
    g_ref[...] += dot_nn(wu_ref[...], gu)
    total = jnp.sum(gu.astype(F32), axis=1, keepdims=True)
    gb_ref[...] = jnp.broadcast_to(total, (total.shape[0], 128)).T[0:8, :]


def branch(half, act_t, act, gd, w_up_t, w_down, w_up, w_down_t, b_col, sums):
    width, rows = act_t.shape
    share = w_down.shape[0] // 2
    steps = share // FF_BLOCK
    down = lambda c, half: (half[0] * steps + c, 0)
    across = lambda c, half: (0, half[0] * steps + c)
    whole = pl.BlockSpec((width, rows), const_map)
    return pl.pallas_call(
        functools.partial(branch_kernel, bool(sums)),
        grid_spec=pltpu.PrefetchScalarGridSpec(
            num_scalar_prefetch=1,
            grid=(steps,),
            in_specs=[
                whole,
                pl.BlockSpec((rows, width), const_map),
                pl.BlockSpec((rows, width), const_map),
                pl.BlockSpec((FF_BLOCK, width), down),
                pl.BlockSpec((FF_BLOCK, width), down),
                pl.BlockSpec((width, FF_BLOCK), across),
                pl.BlockSpec((width, FF_BLOCK), across),
                pl.BlockSpec((FF_BLOCK, 128), down),
            ]
            + [whole] * len(sums),
            out_specs=[
                whole,
                whole,
                pl.BlockSpec((2, FF_BLOCK, width), lambda c, half: (0, c, 0)),
                pl.BlockSpec((8, FF_BLOCK), across),
            ],
        ),
        out_shape=[
            jax.ShapeDtypeStruct((width, rows), F32),
            jax.ShapeDtypeStruct((width, rows), F32),
            jax.ShapeDtypeStruct((2, share, width), BF16),
            jax.ShapeDtypeStruct((8, 2 * share), F32),
        ],
        cost_estimate=cost(12 * rows * width * share, 20 * rows * width, rows * share),
        name="branch",
    )(half, act_t, act, gd, w_up_t, w_down, w_up, w_down_t, b_col, *sums)


def turn_kernel(yt_ref, gt_ref, r_ref, gd_ref, o_ref, w_ref, b_ref, gain_ref, mix_ref, gr_ref, go_ref, gw_ref, sum_ref, acc_ref):
    step = pl.program_id(0)

    @pl.when(step == 0)
    def _():
        acc_ref[...] = jnp.zeros_like(acc_ref)
        sum_ref[...] = jnp.zeros_like(sum_ref)

    r = r_ref[...]
    mix_ref[...] = (r + (yt_ref[...].T + b_ref[...])).astype(BF16)
    grad = gt_ref[...].T
    center, inv = row_stats(r)
    hat = center * inv
    gr = gd_ref[...].astype(F32) + norm_back(grad, hat, inv, gain_ref[...])
    gr_ref[...] = gr
    ga = gr.astype(BF16)
    go_ref[...] = dot_nt(ga, w_ref[...]).astype(BF16)
    acc_ref[...] += dot_nn(o_ref[...].T, ga)
    sum_ref[0:1, :] += jnp.sum(grad * hat, axis=0, keepdims=True)
    sum_ref[1:2, :] += jnp.sum(grad, axis=0, keepdims=True)
    sum_ref[2:3, :] += jnp.sum(ga.astype(F32), axis=0, keepdims=True)

    @pl.when(step == pl.num_programs(0) - 1)
    def _():
        gw_ref[...] = acc_ref[...].astype(BF16)


def turn(y_t, g_t, r, gd, o, w_out, b_down, gain):
    rows, width = r.shape
    blk = lambda i: (i, 0)
    across = lambda i: (0, i)
    row_spec = pl.BlockSpec((ROW_BLOCK, width), blk)
    vec = pl.BlockSpec((1, width), const_map)
    return pl.pallas_call(
        turn_kernel,
        grid=(rows // ROW_BLOCK,),
        in_specs=[
            pl.BlockSpec((width, ROW_BLOCK), across),
            pl.BlockSpec((width, ROW_BLOCK), across),
            row_spec,
            row_spec,
            row_spec,
            pl.BlockSpec((width, width), const_map),
            vec,
            vec,
        ],
        out_specs=[
            row_spec,
            row_spec,
            row_spec,
            pl.BlockSpec((width, width), const_map),
            pl.BlockSpec((8, width), const_map),
        ],
        out_shape=[
            jax.ShapeDtypeStruct((rows, width), BF16),
            jax.ShapeDtypeStruct((rows, width), F32),
            jax.ShapeDtypeStruct((rows, width), BF16),
            jax.ShapeDtypeStruct((width, width), BF16),
            jax.ShapeDtypeStruct((8, width), F32),
        ],
        scratch_shapes=[pltpu.VMEM((width, width), F32)],
        cost_estimate=cost(4 * rows * width * width, 24 * rows * width),
        name="turn",
    )(y_t, g_t, r, gd, o, w_out, b_down, gain)


def project_back_kernel(has_sum, count, at_ref, *refs):
    d_refs, w_ref = refs[:count], refs[count]
    gw_ref, g_ref = refs[-2:]
    d = jnp.concatenate([ref[0] for ref in d_refs], axis=1) if count > 1 else d_refs[0][0]
    gw_ref[...] = dot_nn(at_ref[...], d).astype(BF16)
    term = dot_nt(d, w_ref[...])

    @pl.when(pl.program_id(0) == 0)
    def _():
        g_ref[...] = refs[count + 1][...] + term if has_sum else term

    @pl.when(pl.program_id(0) > 0)
    def _():
        g_ref[...] += term


def project_back(part, act_t, ds, w_qkv, sums):
    width, rows = act_t.shape
    share = sum(d.shape[2] for d in ds)
    whole = pl.BlockSpec((rows, width), const_map)
    return pl.pallas_call(
        functools.partial(project_back_kernel, bool(sums), len(ds)),
        grid=(3,),
        in_specs=[pl.BlockSpec((width, rows), const_map)]
        + [pl.BlockSpec((1, rows, d.shape[2]), lambda i: (i, 0, 0)) for d in ds]
        + [pl.BlockSpec((width, share), lambda i: (0, HEAD_PARTS * i + part))]
        + [whole] * len(sums),
        out_specs=[pl.BlockSpec((width, share), lambda i: (0, i)), whole],
        out_shape=[
            jax.ShapeDtypeStruct((width, 3 * share), BF16),
            jax.ShapeDtypeStruct((rows, width), F32),
        ],
        cost_estimate=cost(12 * rows * width * share, 12 * rows * width),
        name="project_back",
    )(act_t, *ds, w_qkv, *sums)


def leave_kernel(
    mine, order_ref, x_ref, g_ref, gr_ref, gain_ref, turn_ref, down_ref, up0_ref, up1_ref, *rest
):
    qv_refs = rest[:-3]
    back_ref, sum_ref, gx_ref = rest[-3:]
    step = pl.program_id(0)
    rows, width = back_ref.shape

    @pl.when(step == 0)
    def _():
        sum_ref[...] = jnp.zeros_like(sum_ref)
        at = 0
        for ref in qv_refs:
            sum_ref[2:4, at : at + ref.shape[1]] = ref[...]
            at += ref.shape[1]
        sum_ref[4:7, :] = turn_ref[0:3, :]
        sum_ref[7:8, :] = down_ref[...]
        pieces = up0_ref.shape[1] // width
        for n in range(pieces):
            cut = slice(n * width, (n + 1) * width)
            kept = mine[0] == (2 * n) // pieces
            sum_ref[8 + n : 9 + n, :] = jnp.where(kept, up1_ref[0:1, cut], up0_ref[0:1, cut])

    grad = g_ref[...]
    center, inv = row_stats(x_ref[...].astype(F32))
    hat = center * inv
    gx = gr_ref[...] + norm_back(grad, hat, inv, gain_ref[...])
    gx_ref[pl.ds(pl.multiple_of(step * ROW_BLOCK, ROW_BLOCK), ROW_BLOCK), :] = gx.astype(BF16)
    sum_ref[0:1, :] += jnp.sum(grad * hat, axis=0, keepdims=True)
    sum_ref[1:2, :] += jnp.sum(grad, axis=0, keepdims=True)

    @pl.when(step == pl.num_programs(0) - 1)
    def _():
        for r in range(0, rows, ROW_BLOCK):
            spots = lax.broadcasted_iota(jnp.int32, (ROW_BLOCK, rows), 0) + r
            hot = jnp.where(spots == order_ref[...], 1.0, 0.0).astype(BF16)
            back_ref[r : r + ROW_BLOCK, :] = dot_nn(hot, gx_ref[...]).astype(BF16)


def leave(mine, order_row, x, grad, gr, gain, turn_sums, down_bias, up_biases, qvs):
    rows, width = x.shape
    row_spec = pl.BlockSpec((ROW_BLOCK, width), lambda i, m: (i, 0))
    full = lambda v: pl.BlockSpec(v.shape, const_map)
    smalls = (turn_sums, down_bias, *up_biases, *qvs)
    lines = 8 + up_biases[0].shape[1] // width
    lines += -lines % 8
    return pl.pallas_call(
        leave_kernel,
        grid_spec=pltpu.PrefetchScalarGridSpec(
            num_scalar_prefetch=1,
            grid=(rows // ROW_BLOCK,),
            in_specs=[full(order_row), row_spec, row_spec, row_spec, full(gain)]
            + [full(v) for v in smalls],
            out_specs=[
                pl.BlockSpec((rows, width), const_map),
                pl.BlockSpec((lines, width), const_map),
            ],
            scratch_shapes=[pltpu.VMEM((rows, width), BF16)],
        ),
        out_shape=[
            jax.ShapeDtypeStruct((rows, width), BF16),
            jax.ShapeDtypeStruct((lines, width), F32),
        ],
        cost_estimate=cost(2 * rows * rows * width, 12 * rows * width),
        name="leave",
    )(mine, order_row, x, grad, gr, gain, *smalls)


def finish_branch_kernel(bits, down0_ref, down1_ref, up0_ref, up1_ref, down_ref, up_ref):
    def put(down, up):
        down_ref[...] = down[0].astype(F32)
        up_ref[...] = up[0].T.astype(F32)

    mine = pl.program_id(0) == bits[0]
    pl.when(mine)(lambda: put(down0_ref, up0_ref))
    pl.when(jnp.logical_not(mine))(lambda: put(down1_ref, up1_ref))


def finish_branch(bits, downs, ups):
    _, share, width = downs[0].shape
    steps = 4
    cut = share // steps
    own = lambda h, i, b: (0, jnp.where(h == b[0], i, jnp.where(h == 0, 0, steps - 1)), 0)
    far = lambda h, i, b: (0, jnp.where(h != b[0], i, jnp.where(h == 0, 0, steps - 1)), 0)
    blk = (1, cut, width)
    return pl.pallas_call(
        finish_branch_kernel,
        grid_spec=pltpu.PrefetchScalarGridSpec(
            num_scalar_prefetch=1,
            grid=(2, steps),
            in_specs=[
                pl.BlockSpec(blk, own),
                pl.BlockSpec(blk, far),
                pl.BlockSpec(blk, own),
                pl.BlockSpec(blk, far),
            ],
            out_specs=[
                pl.BlockSpec((cut, width), lambda h, i, b: (h * steps + i, 0)),
                pl.BlockSpec((width, cut), lambda h, i, b: (0, h * steps + i)),
            ],
        ),
        out_shape=[
            jax.ShapeDtypeStruct((2 * share, width), F32),
            jax.ShapeDtypeStruct((width, 2 * share), F32),
        ],
        cost_estimate=cost(share * width, 12 * share * width),
        name="finish_branch",
    )(bits, *downs, *ups)


def finish_project_kernel(bits, early0_ref, early1_ref, late0_ref, late1_ref, out_ref, qkv_ref):
    share = out_ref.shape[1] // HEAD_PARTS

    def put(early, late):
        out_ref[...] = early[0].astype(F32)
        for p, part in enumerate((early[1], late[0], late[1])):
            for i in range(3):
                at = (i * HEAD_PARTS + p) * share
                qkv_ref[:, at : at + share] = part[:, i * share : (i + 1) * share].astype(F32)

    mine = pl.program_id(0) == bits[0]
    pl.when(mine)(lambda: put(early0_ref, late0_ref))
    pl.when(jnp.logical_not(mine))(lambda: put(early1_ref, late1_ref))


def finish_project(bits, earlies, lates):
    _, half, width = earlies[0].shape
    steps = 3
    own = lambda h, i, b: (0, jnp.where(h == b[0], i, jnp.where(h == 0, 0, steps - 1)), 0)
    far = lambda h, i, b: (0, jnp.where(h != b[0], i, jnp.where(h == 0, 0, steps - 1)), 0)
    blk = (2, half // steps, width)
    out = lambda h, i, b: (h * steps + i, 0)
    return pl.pallas_call(
        finish_project_kernel,
        grid_spec=pltpu.PrefetchScalarGridSpec(
            num_scalar_prefetch=1,
            grid=(2, steps),
            in_specs=[
                pl.BlockSpec(blk, own),
                pl.BlockSpec(blk, far),
                pl.BlockSpec(blk, own),
                pl.BlockSpec(blk, far),
            ],
            out_specs=[
                pl.BlockSpec((half // steps, width), out),
                pl.BlockSpec((half // steps, 3 * width), out),
            ],
        ),
        out_shape=[
            jax.ShapeDtypeStruct((2 * half, width), F32),
            jax.ShapeDtypeStruct((2 * half, 3 * width), F32),
        ],
        cost_estimate=cost(width * width, 24 * width * width),
        name="finish_project",
    )(bits, *earlies, *lates)


class Links:
    def __init__(self):
        inner = lax.axis_size("dp")
        self.total = lax.axis_size("mod") * inner
        me = lax.axis_index("mod") * inner + lax.axis_index("dp")
        width = self.total.bit_length() - 1
        self.bits = (me >> jnp.arange(width, dtype=jnp.int32)) & 1
        self.me = me
        self.low = list(range(1, inner.bit_length() - 1))
        self.high = list(range(inner.bit_length() - 1, width))

    def swap(self, value, bit):
        pairs = [(i, i ^ (1 << bit)) for i in range(self.total)]
        return lax.ppermute(value, AXES, pairs)

    def half(self, value, other, bit):
        stack, rows, width = value.shape
        side = (self.me >> bit) & 1
        cut = value.reshape(stack, 2, rows // 2, width)
        return lax.dynamic_index_in_dim(cut, 1 - side if other else side, 1, keepdims=False)

    def halve(self, values, bits):
        sends = [self.half(v, True, bit) for v, bit in zip(values, bits)]
        gots = [self.swap(v, bit) for v, bit in zip(sends, bits)]
        keeps = [self.half(v, False, bit) for v, bit in zip(values, bits)]
        return [(k.astype(F32) + g.astype(F32)).astype(BF16) for k, g in zip(keeps, gots)]

    def scatter_sum(self, first, second, small=None):
        values = [first, second]
        for stage, bit in enumerate(self.high):
            twin = self.high[-1 - stage]
            values = self.halve(values, (bit, twin))
            if small is not None and stage == 0:
                for one in [0, *self.high]:
                    small = small + self.swap(small, one)
                *values, small = lax.optimization_barrier((*values, small))
        value = jnp.concatenate(values, axis=0)
        for bit in self.low:
            (value,) = self.halve((value,), (bit,))
        return value if small is None else (value, small)

    def join(self, value, other, bit):
        front = ((self.me >> bit) & 1) == 0
        both = [jnp.where(front, value, other), jnp.where(front, other, value)]
        return jnp.concatenate(both, axis=1)

    def gather(self, value, small=None):
        todo = list(self.low)
        for stage, bit in reversed(list(enumerate(self.low))):
            if small is not None and todo:
                value, small = lax.optimization_barrier((value, small))
                small = small + self.swap(small, todo.pop())
            other = self.swap(value, bit)
            value = self.join(value, other, bit)
        while small is not None and todo:
            small = small + self.swap(small, todo.pop())
        if small is not None:
            value, small = lax.optimization_barrier((value, small))
        values = jnp.split(value, 2, axis=0)
        for stage, bit in reversed(list(enumerate(self.high))):
            bits = (bit, self.high[-1 - stage])
            others = [self.swap(v, b) for v, b in zip(values, bits)]
            values = [self.join(v, w, b) for v, w, b in zip(values, others, bits)]
        pairs = [(v, self.swap(v, 0)) for v in values]
        return pairs if small is None else (*pairs, small)


def on_device(
    tokens,
    token_order,
    item_ids,
    step_blocks,
    item_sets,
    action_mask,
    cotangent,
    ln1_gain,
    ln1_bias,
    w_qkv,
    b_qv,
    w_out,
    b_out,
    ln2_gain,
    ln2_bias,
    w_up,
    b_up,
    w_down,
    b_down,
):
    rows, width = tokens.shape
    quarter_rows = rows // lax.axis_size("mod")
    links = Links()
    arrived = lax.all_to_all(tokens, AXES, split_axis=0, concat_axis=0, tiled=True)

    tok_order = token_order[0]
    segment = item_ids[0]
    code = segment * 2 + step_blocks[0]
    code_row = code[None, :]
    code_col = jnp.broadcast_to(code[:, None], (rows, 128))
    order_col = jnp.broadcast_to(tok_order[:, None], (rows, 128))
    tab = window_table(segment, rows)
    item_hot = segment[:, None] == jnp.arange(item_sets.shape[1], dtype=jnp.int32)[None, :]
    set_row = jnp.sum(jnp.where(item_hot, item_sets[0][None, :], 0), axis=1)
    set_hot = (
        set_row[:, None] == jnp.arange(action_mask.shape[0], dtype=jnp.int32)[None, :]
    ).astype(F32)
    mask_rows = jnp.dot(set_hot, action_mask.astype(F32))
    modality = tok_order // quarter_rows
    mod_hot = (
        modality[:, None] == jnp.arange(action_mask.shape[1], dtype=jnp.int32)[None, :]
    ).astype(F32)
    select = jnp.sum(mask_rows * mod_hot, axis=1)
    grad_down = (cotangent.astype(F32) * select[:, None]).astype(BF16)
    g_down_bias = jnp.sum(grad_down.astype(F32), axis=0)[None, :]

    row = lambda v: v.astype(F32)[None, :]
    gain_one, shift_one = row(ln1_gain), row(ln1_bias)
    gain_two, shift_two = row(ln2_gain), row(ln2_bias)
    bias_qv = b_qv.astype(F32)
    bias_qkv = jnp.concatenate([bias_qv[0], jnp.zeros((width,), F32), bias_qv[1]])[None, :]
    b_col = jnp.broadcast_to(b_up.astype(F32)[:, None], (b_up.shape[0], 128))
    w_up_t = w_up.T
    w_down_t = w_down.T

    x, act_t, qkv = enter(order_col, arrived, gain_one, shift_one, w_qkv, bias_qkv)
    attn, lse = attend(qkv, tab, code_row, code_col)
    r, act2, act2_t = middle(attn, x, w_out, row(b_out), gain_two, shift_two)
    bits = links.bits
    mine = bits[0:1]
    sums, halves, biases = (), [], []
    for half in (1 - mine, mine):
        y_t, g_t, g_pair, g_bias = branch(
            half, act2_t, act2, grad_down, w_up_t, w_down, w_up, w_down_t, b_col, sums
        )
        sums = (y_t, g_t)
        halves.append(g_pair)
        biases.append(g_bias)
    got = links.swap(halves[0], 0)
    g_pair = (halves[1].astype(F32) + got.astype(F32)).astype(BF16)
    downs, ups = links.gather(links.scatter_sum(g_pair[:1], g_pair[1:]))
    g_down, g_up = finish_branch(bits, downs, ups)
    mixed_out, gr, go, g_out, turn_sums = turn(
        y_t, g_t, r, grad_down, attn, w_out, row(b_down), gain_two
    )
    sums = ()
    units, qv_parts = [g_out], []
    for part, runs in enumerate(((2,), (2,), (1, 1))):
        ds, at = [], 2 * part
        for count in runs:
            d, qv = attend_back(at, count, qkv, go, lse, tab, code_row, code_col)
            at += count
            ds.append(d)
            qv_parts.append(qv)
        g_qkv, grad = project_back(part, act_t, ds, w_qkv, sums)
        sums = (grad,)
        units.append(g_qkv)
    (pairs,) = links.halve((jnp.stack(units),), (0,))
    back, small = leave(
        mine, token_order, x, grad, gr, gain_one, turn_sums, g_down_bias, biases, qv_parts
    )
    token_grad = lax.all_to_all(back, AXES, split_axis=0, concat_axis=0, tiled=True)
    total, small = links.scatter_sum(pairs[:2], pairs[2:], small)
    earlies, lates, small = links.gather(total, small)
    g_out, g_qkv = finish_project(bits, earlies, lates)
    lines = b_up.shape[0] // width
    return (
        mixed_out,
        token_grad,
        small[0],
        small[1],
        g_qkv,
        small[2:4],
        g_out,
        small[6],
        small[4],
        small[5],
        g_up,
        small[8 : 8 + lines].reshape(-1),
        g_down,
        small[7],
    )


def solution(mesh):
    split = P(AXES, None)
    in_specs = (split,) * 5 + (P(), split) + (P(),) * 12
    out_specs = (split, split) + (P(),) * 12

    return jax.shard_map(
        on_device, mesh=mesh, in_specs=in_specs, out_specs=out_specs, check_vma=False
    )
```
